128 devices in a mesh: grp: 8 (over z_lo, y), dev: 16 (over z_hi, x, core).
Axes of the slice: x: 4, y: 4, z: 4 (z_hi: 2, z_lo: 2; z = z_hi * 2 + z_lo), core: 2. Of those that a mesh axis runs over, the one named last changes fastest.
Arguments:
- fine_nodes: bfloat16 [327680, 512], P(('grp', 'dev')), may hold values from -6 to 6
- mid_nodes: bfloat16 [81920, 512], P(('grp', 'dev')), may hold values from -6 to 6
- coarse_nodes: bfloat16 [20480, 512], P('dev'), may hold values from -6 to 6
- fine_owner: int32 [327680, 1], P(('grp', 'dev')), may hold values from 0 to 127, as said below
- fine_parent: int32 [327680], P(('grp', 'dev')), may hold values from 0 to 639
- mid_owner: int32 [81920, 1], P(('grp', 'dev')), may hold values from 0 to 15, as said below
- mid_parent: int32 [81920], P(('grp', 'dev')), may hold values from 0 to 1279
- neighbours: int32 [20480, 6], P('dev'), may hold values from 0 to 20479, as said below
- neighbour_mask: int32 [20480, 6], P('dev'), may hold values from 0 to 1, as said below
- up_child_w: bfloat16 [512, 512], replicated, may hold values from -0.25 to 0.25
- up_parent_w: bfloat16 [512, 512], replicated, may hold values from -0.25 to 0.25
- up_out_w: bfloat16 [512, 512], replicated, may hold values from -0.25 to 0.25
- up_bias: float32 [512], replicated, may hold values from -3 to 3
- up_gain: float32 [512], replicated, may hold values from 0.1 to 1.9
- mid_child_w: bfloat16 [512, 512], replicated, may hold values from -0.25 to 0.25
- mid_parent_w: bfloat16 [512, 512], replicated, may hold values from -0.25 to 0.25
- mid_out_w: bfloat16 [512, 512], replicated, may hold values from -0.25 to 0.25
- mid_bias: float32 [512], replicated, may hold values from -3 to 3
- mid_gain: float32 [512], replicated, may hold values from 0.1 to 1.9
- same_self_w: bfloat16 [512, 512], replicated, may hold values from -0.25 to 0.25
- same_other_w: bfloat16 [512, 512], replicated, may hold values from -0.25 to 0.25
- same_out_w: bfloat16 [512, 512], replicated, may hold values from -0.25 to 0.25
- same_bias: float32 [512], replicated, may hold values from -3 to 3
- same_gain: float32 [512], replicated, may hold values from 0.1 to 1.9
- down_child_w: bfloat16 [512, 512], replicated, may hold values from -0.25 to 0.25
- down_parent_w: bfloat16 [512, 512], replicated, may hold values from -0.25 to 0.25
- down_out_w: bfloat16 [512, 512], replicated, may hold values from -0.25 to 0.25
- down_bias: float32 [512], replicated, may hold values from -3 to 3
- down_gain: float32 [512], replicated, may hold values from 0.1 to 1.9
Outputs:
- mid_out: bfloat16 [81920, 512], P(('grp', 'dev'))
- coarse_out: bfloat16 [20480, 512], P('dev')
The draws below stay inside these ranges and needn't reach their ends.
Inputs may be any that keep to these rules, and one draw needn't show every extreme that they name: `fine_owner`: each device's rows name that device itself or one of the four devices up to two places away along grp+dev, counted around the end. No device other than itself is named more than 320 times from one device's rows, and every device's rows name one of them exactly 320 times. `mid_owner`: the rows of the device at index d of dev name d or an index up to two places away from d along dev, counted around the end. No index other than d is named more than 80 times from one device's rows, and every device's rows name one of them exactly 80 times. `neighbours`: row i names rows within 1280 places of i, counted around the end of the 20480 rows, never i itself. `neighbour_mask`: exactly 12 rows have one unused slot, the last one; all other slots are used.
All inputs are finite; a program needn't handle non-finite values.
Results may differ from the reference program's by a relative error of at most 0.01.
Values may be sent and summed in bfloat16 or wider, within the bound.
No kernel may reach another device: no remote copies, remote signals or barrier semaphores. Data moves between devices by JAX's collectives and lax.ppermute only.
A program may use at most 128 MiB of HBM per device.

```python
import jax
import jax.numpy as jnp
from jax import lax

W = 512
HID = 512
K = 6
F0 = 2560
F1 = 640
F2 = 1280
CAP0 = 320
CAP1 = 80
N0 = 327680
N1 = 81920
N2 = 20480


def shuffle_block(seed_key, block):
    return jax.random.permutation(seed_key, block)


def spill_offsets(key, blocks, block, capacity):
    first, second, third = jax.random.split(key, 3)
    counts = jax.random.randint(first, (blocks, 4), capacity // 4, capacity + 1, dtype=jnp.int32)
    chosen = jax.random.randint(second, (blocks,), 0, 4, dtype=jnp.int32)
    counts = jnp.where(jnp.arange(4, dtype=jnp.int32)[None, :] == chosen[:, None], capacity, counts)
    ends = jnp.cumsum(counts, axis=1)
    places = jnp.arange(block, dtype=jnp.int32)
    which = jnp.sum((places[None, :, None] >= ends[:, None, :]).astype(jnp.int32), axis=2)
    moves = jnp.array([-2, -1, 1, 2, 0], jnp.int32)
    offset = jnp.take(moves, which, axis=0)
    orders = jax.vmap(lambda seed_key: shuffle_block(seed_key, block))(jax.random.split(third, blocks))
    return jnp.take_along_axis(offset, orders.astype(jnp.int32), axis=1)


def draw_fine_owner(key, part):
    blocks = N0 // F0
    offset = spill_offsets(jax.random.fold_in(key, 11), blocks, F0, CAP0)
    device = jnp.arange(blocks, dtype=jnp.int32)[:, None]
    return ((device + offset) % blocks).reshape(N0, 1).astype(jnp.int32)


def draw_mid_owner(key, part):
    blocks = N1 // F1
    members = N2 // F2
    offset = spill_offsets(jax.random.fold_in(key, 23), blocks, F1, CAP1)
    device = (jnp.arange(blocks, dtype=jnp.int32) % members)[:, None]
    return ((device + offset) % members).reshape(N1, 1).astype(jnp.int32)


def draw_neighbours(key, part):
    first, second = jax.random.split(jax.random.fold_in(key, 37))
    across = jax.random.randint(first, (N2, K), 1, F2 + 1, dtype=jnp.int32)
    direction = jax.random.randint(second, (N2, K), 0, 2, dtype=jnp.int32) * 2 - 1
    places = jnp.arange(N2, dtype=jnp.int32)[:, None]
    return ((places + direction * across) % N2).astype(jnp.int32)


def draw_neighbour_mask(key, part):
    picked = jax.random.permutation(jax.random.fold_in(key, 41), N2)[:12].astype(jnp.int32)
    places = jnp.arange(N2, dtype=jnp.int32)
    struck = jnp.any(places[:, None] == picked[None, :], axis=1)
    last = jnp.arange(K, dtype=jnp.int32)[None, :] == K - 1
    return jnp.where(struck[:, None] & last, 0, 1).astype(jnp.int32)


def set_ends(result, own_key, smallest, high):
    spot = [jax.random.randint(jax.random.fold_in(own_key, axis), (), 0, length) for axis, length in enumerate(result.shape)]
    longest = result.shape.index(max(result.shape))
    neighbour = spot[:longest] + [(spot[longest] + 1) % result.shape[longest]] + spot[longest + 1:]
    return result.at[tuple(spot)].set(smallest).at[tuple(neighbour)].set(high)


def block_levels(stream_key, shape, shards, least, high):
    loudness = 1.0
    for position, parts in shards:
        draws = jax.random.uniform(jax.random.fold_in(jax.random.fold_in(stream_key, 6), position), (parts,), jnp.float32, least / len(shards), high / len(shards))
        loudness = loudness * jnp.repeat(jnp.exp(draws), shape[position] // parts).reshape((-1,) + (1,) * (len(shape) - 1 - position))
    return loudness


def scatter_about(own_key, dims, scale, most, shards=(), kind=jnp.bfloat16):
    values = scale * jax.random.normal(own_key, dims, jnp.float32)
    if shards:
        values = values * block_levels(own_key, dims, shards, -0.22, 0.18)
    return jnp.clip(values, -most, most).astype(kind)


def setup_inputs(seed: int = 0) -> dict:
    key_list = jax.random.split(jax.random.key(seed), 30)
    fine_nodes = scatter_about(key_list[0], (N0, W), 1.0, 6.0, ((0, 128),))
    mid_nodes = scatter_about(key_list[1], (N1, W), 1.0, 6.0, ((0, 128),))
    coarse_nodes = scatter_about(key_list[2], (N2, W), 1.0, 6.0, ((0, 16),))
    fine_owner = draw_fine_owner(jax.random.fold_in(key_list[29], 71), 0)
    fine_parent = set_ends(jax.random.randint(key_list[4], (N0,), 0, F1), jax.random.fold_in(key_list[4], 1), 0, F1 - 1).astype(jnp.int32)
    mid_owner = draw_mid_owner(jax.random.fold_in(key_list[29], 71), 0)
    mid_parent = set_ends(jax.random.randint(key_list[6], (N1,), 0, F2), jax.random.fold_in(key_list[6], 1), 0, F2 - 1).astype(jnp.int32)
    neighbours = draw_neighbours(jax.random.fold_in(key_list[29], 71), 0)
    neighbour_mask = draw_neighbour_mask(jax.random.fold_in(key_list[29], 71), 0)
    up_child_w = scatter_about(key_list[9], (W, HID), W ** -0.5, 0.25)
    up_parent_w = scatter_about(key_list[10], (W, HID), W ** -0.5, 0.25)
    up_out_w = scatter_about(key_list[11], (HID, W), HID ** -0.5, 0.25)
    up_bias = scatter_about(key_list[12], (HID,), 0.5, 3.0, (), jnp.float32)
    up_gain = jnp.clip(1.0 + 0.18 * jax.random.normal(key_list[13], (W,), jnp.float32), 0.1, 1.9)
    mid_child_w = scatter_about(key_list[14], (W, HID), W ** -0.5, 0.25)
    mid_parent_w = scatter_about(key_list[15], (W, HID), W ** -0.5, 0.25)
    mid_out_w = scatter_about(key_list[16], (HID, W), HID ** -0.5, 0.25)
    mid_bias = scatter_about(key_list[17], (HID,), 0.5, 3.0, (), jnp.float32)
    mid_gain = jnp.clip(1.0 + 0.18 * jax.random.normal(key_list[18], (W,), jnp.float32), 0.1, 1.9)
    same_self_w = scatter_about(key_list[19], (W, HID), W ** -0.5, 0.25)
    same_other_w = scatter_about(key_list[20], (W, HID), W ** -0.5, 0.25)
    same_out_w = scatter_about(key_list[21], (HID, W), HID ** -0.5, 0.25)
    same_bias = scatter_about(key_list[22], (HID,), 0.5, 3.0, (), jnp.float32)
    same_gain = jnp.clip(1.0 + 0.18 * jax.random.normal(key_list[23], (W,), jnp.float32), 0.1, 1.9)
    down_child_w = scatter_about(key_list[24], (W, HID), W ** -0.5, 0.25)
    down_parent_w = scatter_about(key_list[25], (W, HID), W ** -0.5, 0.25)
    down_out_w = scatter_about(key_list[26], (HID, W), HID ** -0.5, 0.25)
    down_bias = scatter_about(key_list[27], (HID,), 0.5, 3.0, (), jnp.float32)
    down_gain = jnp.clip(1.0 + 0.18 * jax.random.normal(key_list[28], (W,), jnp.float32), 0.1, 1.9)
    return dict(fine_nodes=fine_nodes, mid_nodes=mid_nodes, coarse_nodes=coarse_nodes, fine_owner=fine_owner, fine_parent=fine_parent, mid_owner=mid_owner, mid_parent=mid_parent, neighbours=neighbours, neighbour_mask=neighbour_mask, up_child_w=up_child_w, up_parent_w=up_parent_w, up_out_w=up_out_w, up_bias=up_bias, up_gain=up_gain, mid_child_w=mid_child_w, mid_parent_w=mid_parent_w, mid_out_w=mid_out_w, mid_bias=mid_bias, mid_gain=mid_gain, same_self_w=same_self_w, same_other_w=same_other_w, same_out_w=same_out_w, same_bias=same_bias, same_gain=same_gain, down_child_w=down_child_w, down_parent_w=down_parent_w, down_out_w=down_out_w, down_bias=down_bias, down_gain=down_gain)


def layer_norm(values, gain):
    center = values - lax.optimization_barrier(jnp.mean(values, axis=-1, keepdims=True))
    spread = lax.optimization_barrier(jnp.mean(center * center, axis=-1, keepdims=True))
    return center * lax.rsqrt(spread + 1e-05) * gain

def edge_rows(child_rows, parent_rows, w_child, w_out, bias):
    hidden = jax.nn.silu(jnp.dot(child_rows, w_child, preferred_element_type=jnp.float32) + parent_rows + bias)
    return jnp.dot(hidden.astype(jnp.bfloat16), w_out, preferred_element_type=jnp.float32)

def reference(fine_nodes, mid_nodes, coarse_nodes, fine_owner, fine_parent, mid_owner, mid_parent, neighbours, neighbour_mask, up_child_w, up_parent_w, up_out_w, up_bias, up_gain, mid_child_w, mid_parent_w, mid_out_w, mid_bias, mid_gain, same_self_w, same_other_w, same_out_w, same_bias, same_gain, down_child_w, down_parent_w, down_out_w, down_bias, down_gain):
    fine_target = (fine_owner[:, 0] * F1 + fine_parent).astype(jnp.int32)
    mid_terms = jnp.dot(mid_nodes, up_parent_w, preferred_element_type=jnp.float32)

    def fine_block(pair):
        rows, target = pair
        return edge_rows(rows, jnp.take(mid_terms, target, axis=0), up_child_w, up_out_w, up_bias).astype(jnp.bfloat16)
    blocks = N0 // F0
    fine_messages = lax.map(fine_block, (fine_nodes.reshape(blocks, F0, W), fine_target.reshape(blocks, F0)))
    fine_sum = jax.ops.segment_sum(fine_messages.reshape(N0, W).astype(jnp.float32), fine_target, num_segments=N1)
    mid_update = (mid_nodes.astype(jnp.float32) + layer_norm(fine_sum, up_gain)).astype(jnp.bfloat16)
    mid_target = (mid_owner[:, 0] * F2 + mid_parent).astype(jnp.int32)
    coarse_terms = jnp.dot(coarse_nodes, mid_parent_w, preferred_element_type=jnp.float32)
    mid_messages = edge_rows(mid_update, jnp.take(coarse_terms, mid_target, axis=0), mid_child_w, mid_out_w, mid_bias).astype(jnp.bfloat16)
    coarse_sum = jax.ops.segment_sum(mid_messages.astype(jnp.float32), mid_target, num_segments=N2)
    coarse_update = (coarse_nodes.astype(jnp.float32) + layer_norm(coarse_sum, mid_gain)).astype(jnp.bfloat16)
    self_terms = jnp.dot(coarse_update, same_self_w, preferred_element_type=jnp.float32)
    other_terms = jnp.dot(coarse_update, same_other_w, preferred_element_type=jnp.float32).astype(jnp.bfloat16)
    picked = jnp.take(other_terms, neighbours.reshape(-1), axis=0).reshape(N2, K, HID)
    same_hidden = jax.nn.silu(self_terms[:, None, :] + picked.astype(jnp.float32) + same_bias).astype(jnp.bfloat16)
    message = jnp.dot(same_hidden.reshape(N2 * K, HID), same_out_w, preferred_element_type=jnp.float32).reshape(N2, K, W)
    same_sum = lax.optimization_barrier(jnp.sum(message * neighbour_mask[:, :, None].astype(jnp.float32), axis=1))
    coarse_out = (coarse_update.astype(jnp.float32) + layer_norm(same_sum, same_gain)).astype(jnp.bfloat16)
    down_terms = jnp.dot(coarse_out, down_parent_w, preferred_element_type=jnp.float32).astype(jnp.bfloat16)
    parent_rows = jnp.take(down_terms, mid_target, axis=0).astype(jnp.float32)
    down_messages = edge_rows(mid_update, parent_rows, down_child_w, down_out_w, down_bias)
    mid_out = (mid_update.astype(jnp.float32) + layer_norm(down_messages, down_gain)).astype(jnp.bfloat16)
    return (mid_out, coarse_out)
```

```python
import functools

import jax
import jax.numpy as jnp
from jax import lax
from jax.experimental import pallas as pl
from jax.experimental.pallas import tpu as pltpu
from jax.sharding import PartitionSpec as P

F32 = jnp.float32
BF16 = jnp.bfloat16
I32 = jnp.int32
OFFSETS = (-2, -1, 1, 2)


def dot(a, b):
    return jnp.dot(a, b, preferred_element_type=F32)


def iota(shape, dim):
    return lax.broadcasted_iota(I32, shape, dim)


def one_hot(hit):
    return jnp.where(hit, 1.0, 0.0).astype(BF16)


def columns_of(row):
    return jnp.transpose(jnp.broadcast_to(row, (128, row.shape[1])))


def pick(cols, count):
    lanes = iota(cols.shape, 1)
    return jnp.concatenate([one_hot(cols == lanes + 128 * j) for j in range(count // 128)], axis=1)


def member(row, count):
    return one_hot(iota((count, row.shape[1]), 0) == row)


def silu(v):
    half = 0.5 * v
    return half + half * jnp.tanh(half)


def layer_norm(values, gain):
    center = values - jnp.mean(values, axis=-1, keepdims=True)
    spread = jnp.mean(center * center, axis=-1, keepdims=True)
    return center * lax.rsqrt(spread + 1e-05) * gain


def digits(row):
    high = jnp.floor(row * (1.0 / 256.0))
    low = row - 256.0 * high
    wide = (8, row.shape[1])
    return jnp.concatenate([jnp.broadcast_to(high, wide), jnp.broadcast_to(low, wide)], axis=0).astype(BF16)


def undigits(block):
    values = block.astype(F32)
    return values[0:1] * 256.0 + values[8:9]


def relative_owner(owner, me, total):
    rel = owner - me
    return jnp.where(rel < 0, rel + total, rel)


def places(rel, total, columns, chunk):
    lanes = rel.shape[1]
    subl = iota((8, lanes), 0)
    code = jnp.full((8, lanes), -5, I32)
    for r, c in enumerate(columns):
        code = jnp.where(subl == r, OFFSETS[c] % total, code)
    chosen = jnp.where(rel == code, 1.0, 0.0)
    parts = lanes // chunk
    stacked = jnp.concatenate([chosen[:, chunk * j : chunk * (j + 1)] for j in range(parts)], axis=0)
    below = one_hot(iota((chunk, chunk), 0) < iota((chunk, chunk), 1))
    before = dot(stacked.astype(BF16), below)
    totals = jnp.sum(stacked, axis=1, keepdims=True)
    offset = jnp.zeros((8, 1), F32)
    out = []
    for j in range(parts):
        rows = slice(8 * j, 8 * j + 8)
        out.append(jnp.where(stacked[rows] > 0, before[rows] + offset, -1.0))
        offset = offset + totals[rows]
    return out


def my_index(members):
    return lax.axis_index("grp") * members + lax.axis_index("dev")


def pack_fine(owner, parent, nodes, *rest, columns, everyone, members, capacity):
    outs, picked = rest[: len(columns)], rest[len(columns)]
    rel = relative_owner(owner[...], my_index(members), everyone)
    place = places(rel, everyone, columns, 256)
    label = parent[...].astype(F32) + 1.0
    for r, c in enumerate(columns):
        total = jnp.zeros((capacity, 128), F32)
        for j, part in enumerate(place):
            hit = part[r : r + 1].astype(I32) == iota((capacity, 256), 0)
            picked[:, 256 * j : 256 * (j + 1)] = one_hot(hit)
            marked = jnp.where(hit, label[:, 256 * j : 256 * (j + 1)], 0.0)
            total = total + marked[:, :128] + marked[:, 128:]
        shift = (capacity * c) % 128
        spare = jnp.zeros((64, 128), F32)
        total = jnp.concatenate([spare, total] if shift else [total, spare], axis=0)
        row = jnp.sum(jnp.transpose(total), axis=0, keepdims=True)
        outs[r][0:capacity, :] = dot(picked[...], nodes[...]).astype(BF16)
        outs[r][capacity : capacity + 16, 0 : capacity + 64] = digits(row)


def fine_own(owner, parent, nodes, mids, w_parent, w_child, bias, total, terms, *, everyone, members):
    @pl.when(pl.program_id(0) == 0)
    def _():
        terms[...] = dot(mids[...], w_parent[...]).astype(BF16)
        total[...] = jnp.zeros_like(total)

    rel = relative_owner(owner[...], my_index(members), everyone)
    label = jnp.where(rel == 0, parent[...], -1)
    count = terms.shape[0]
    before = dot(nodes[...], w_child[...]) + dot(pick(columns_of(label), count), terms[...]) + bias[...]
    total[...] += dot(member(label, count), silu(before).astype(BF16))


def fine_received(
    m0, m1, m2, m3, terms, own_sum, w_child, bias, w_out, gain, mids, owner, parent,
    update, p0, p1, p2, p3, hidden, *, members, capacity, mid_capacity,
):
    count = terms.shape[0]
    rows = []
    for c, m in enumerate((m0, m1, m2, m3)):
        row = undigits(m[capacity : capacity + 16, 0 : capacity + 64]) - 1.0
        cols = columns_of(row.astype(I32))
        shift = (capacity * c) % 128
        cols = cols[shift : shift + capacity]
        before = dot(m[0:capacity, :], w_child[...]) + dot(pick(cols, count), terms[...]) + bias[...]
        hidden[capacity * c : capacity * (c + 1), :] = silu(before).astype(BF16)
        rows.append(row + 1.0)
    total = own_sum[...]
    for h in range(2):
        a, b = rows[2 * h], rows[2 * h + 1]
        row = jnp.concatenate([a[:, :256], a[:, 256:] + b[:, :128], b[:, 128:]], axis=1) - 1.0
        total = total + dot(member(row.astype(I32), count), hidden[2 * capacity * h : 2 * capacity * (h + 1), :])
    fine_sum = dot(total.astype(BF16), w_out[...])
    new = (mids[...].astype(F32) + layer_norm(fine_sum, gain[...])).astype(BF16)
    update[...] = new
    rel = relative_owner(owner[...], lax.axis_index("dev"), members)
    place = places(rel, members, (0, 1, 2, 3), 128)
    slots = 4 * mid_capacity
    labels = parent[...].astype(F32) + 1.0
    picked, marks = [], jnp.zeros((slots, 128), F32)
    for j, part in enumerate(place):
        base = iota((8, 128), 0).astype(F32) * float(mid_capacity)
        slot = jnp.max(jnp.where(part >= 0, part + base, -1.0), axis=0, keepdims=True)
        hit = slot.astype(I32) == iota((slots, 128), 0)
        picked.append(one_hot(hit))
        marks = marks + jnp.where(hit, labels[:, 128 * j : 128 * (j + 1)], 0.0)
    marks = jnp.concatenate([marks, jnp.zeros((384 - slots, 128), F32)], axis=0)
    code = digits(jnp.sum(jnp.transpose(marks), axis=0, keepdims=True))
    out = dot(jnp.concatenate(picked, axis=1), new).astype(BF16)
    for c, p in enumerate((p0, p1, p2, p3)):
        p[0:mid_capacity, :] = out[mid_capacity * c : mid_capacity * (c + 1)]
        p[mid_capacity : mid_capacity + 16, 0:384] = code


def mid_own(owner, parent, update, coarse, w_parent, w_child, bias, total, terms, *, members):
    terms[...] = dot(coarse[...], w_parent[...]).astype(BF16)
    rel = relative_owner(owner[...], lax.axis_index("dev"), members)
    label = jnp.where(rel == 0, parent[...], -1)
    count = terms.shape[0]
    before = dot(update[...], w_child[...]) + dot(pick(columns_of(label), count), terms[...]) + bias[...]
    total[...] = dot(member(label, count), silu(before).astype(BF16))


def mid_received(m0, m1, m2, m3, terms, own_sum, w_child, bias, *rest, groups, capacity):
    shares, labels, rows, total = rest[:groups], rest[groups], rest[groups + 1], rest[groups + 2]
    count = terms.shape[0]
    lanes = iota((1, 384), 1)
    label = jnp.zeros((1, 384), F32)
    for c, m in enumerate((m0, m1, m2, m3)):
        rows[capacity * c : capacity * (c + 1), :] = m[0:capacity, :]
        row = undigits(m[capacity : capacity + 16, 0:384])
        mine = (lanes >= capacity * c) & (lanes < capacity * (c + 1))
        label = label + jnp.where(mine, row, 0.0)
    label = (label - 1.0).astype(I32)
    labels[...] = jnp.broadcast_to(label, labels.shape)
    slots = 4 * capacity
    cols = columns_of(label)[0:slots]
    before = dot(rows[...], w_child[...]) + dot(pick(cols, count), terms[...]) + bias[...]
    total[...] = own_sum[...] + dot(member(label[:, 0:slots], count), silu(before).astype(BF16))
    share = count // groups
    g = lax.axis_index("grp")
    for j, out in enumerate(shares):
        at = lax.rem(g + j, groups) * share
        out[...] = total[pl.ds(pl.multiple_of(at, 16), share), :].astype(BF16)


def coarse_mine(*refs, groups):
    pieces = refs[:groups]
    coarse, w_out, gain, w_self, w_other, bias, update, own_terms, other = refs[groups:]
    total = pieces[0][...].astype(F32)
    for p in pieces[1:]:
        total = total + p[...].astype(F32)
    coarse_sum = dot(total.astype(BF16), w_out[...])
    share = update.shape[0]
    at = pl.multiple_of(lax.axis_index("grp") * share, 16)
    new = (coarse[pl.ds(at, share), :].astype(F32) + layer_norm(coarse_sum, gain[...])).astype(BF16)
    update[...] = new
    other[...] = dot(new, w_other[...]).astype(BF16)
    own_terms[...] = dot(new, w_self[...]) + bias[...]


def same_level(*refs, groups, members):
    blocks = refs[: 2 * groups + 1]
    near, mask, own_terms, update, w_out, gain, result, window = refs[2 * groups + 1 :]
    share = result.shape[0]
    count = groups * share
    g, d = lax.axis_index("grp"), lax.axis_index("dev")
    window[0:share, :] = blocks[1][...]
    window[count : count + share, :] = blocks[0][...]
    window[2 * count : 2 * count + share, :] = blocks[2][...]
    for s in range(1, groups):
        wrap = (g + s >= groups).astype(I32)
        same, side = blocks[2 + s], blocks[groups + 1 + s]
        at = s * share + count * (1 - wrap)
        window[pl.ds(pl.multiple_of(at, 16), share), :] = same[...]
        at = s * share + count * wrap
        window[pl.ds(pl.multiple_of(at, 16), share), :] = side[...]
    own = pl.ds(pl.multiple_of(g * share, 8), share)
    ids = near[own, :]
    used = mask[own, :].astype(F32)
    local = ids - (d * count + g * share - count)
    whole = members * count
    local = jnp.where(local < 0, local + whole, local)
    local = jnp.where(local >= whole, local - whole, local)
    span = window.shape[0]
    last = 2 * count + share
    window[last:span, :] = jnp.zeros((span - last, window.shape[1]), BF16)
    hidden = jnp.zeros((share, result.shape[1]), F32)
    for k in range(near.shape[1]):
        cols = jnp.broadcast_to(local[:, k : k + 1], (share, 128))
        lanes = iota(cols.shape, 1)
        picks = [one_hot(cols == lanes + 128 * j) for j in range(span // 128)]
        got = dot(jnp.concatenate(picks, axis=1), window[...])
        h = silu(own_terms[...] + got).astype(BF16).astype(F32)
        hidden = hidden + used[:, k : k + 1] * h
    same_sum = dot(hidden.astype(BF16), w_out[...])
    result[...] = (update[...].astype(F32) + layer_norm(same_sum, gain[...])).astype(BF16)


def coarse_joined(*refs, groups, capacity):
    pieces = refs[:groups]
    labels, result, r0, r1, r2, r3 = refs[groups:]
    share = pieces[0].shape[0]
    g = lax.axis_index("grp")
    for s, p in enumerate(pieces):
        at = lax.rem(g + s, groups) * share
        result[pl.ds(pl.multiple_of(at, 16), share), :] = p[...]
    cols = columns_of(labels[0:1, :])[0 : 4 * capacity]
    rows = dot(pick(cols, result.shape[0]), result[...]).astype(BF16)
    for c, r in enumerate((r0, r1, r2, r3)):
        r[...] = rows[capacity * c : capacity * (c + 1)]


def down_own(owner, parent, coarse, update, w_parent, w_child, bias, result, *, members):
    rel = relative_owner(owner[...], lax.axis_index("dev"), members)
    label = jnp.where(rel == 0, parent[...], -1)
    rows = dot(pick(columns_of(label), coarse.shape[0]), coarse[...]).astype(BF16)
    terms = dot(rows, w_parent[...]).astype(BF16).astype(F32)
    result[...] = dot(update[...], w_child[...]) + terms + bias[...]


def down_received(r0, r1, r2, r3, owner, own_terms, update, w_parent, w_out, gain, result, rows, *, members, capacity):
    for c, r in enumerate((r0, r1, r2, r3)):
        rows[capacity * c : capacity * (c + 1), :] = r[...]
    slots = 4 * capacity
    terms = dot(rows[...], w_parent[...]).astype(BF16)
    rel = relative_owner(owner[...], lax.axis_index("dev"), members)
    place = places(rel, members, (0, 1, 2, 3), 128)
    back = []
    for part in place:
        base = iota((8, 128), 0).astype(F32) * float(capacity)
        slot = jnp.max(jnp.where(part >= 0, part + base, -1.0), axis=0, keepdims=True)
        cols = columns_of(slot.astype(I32))
        wide = jnp.concatenate([cols, cols, cols], axis=1)[:, 0:slots]
        back.append(one_hot(wide == iota((128, slots), 1)))
    before = own_terms[...] + dot(jnp.concatenate(back, axis=0), terms)
    messages = dot(silu(before).astype(BF16), w_out[...])
    result[...] = (update[...].astype(F32) + layer_norm(messages, gain[...])).astype(BF16)


def shape(rows, width, kind=BF16):
    return jax.ShapeDtypeStruct((rows, width), kind)


def call(body, outs, args, scratch=(), flops=0, name=None, **static):
    moved = sum(a.size * a.dtype.itemsize for a in (*args, *outs))
    return pl.pallas_call(
        functools.partial(body, **static),
        out_shape=outs,
        in_specs=[pl.BlockSpec(memory_space=pltpu.VMEM)] * len(args),
        out_specs=[pl.BlockSpec(memory_space=pltpu.VMEM)] * len(outs),
        scratch_shapes=list(scratch),
        cost_estimate=pl.CostEstimate(flops=flops, bytes_accessed=moved, transcendentals=0),
        name=name or body.__name__,
    )(*args)


def from_behind(value, axis, steps):
    count = lax.axis_size(axis)
    return lax.ppermute(value, axis, [(s, (s + steps) % count) for s in range(count)])


def on_device(
    fine_nodes, mid_nodes, coarse_nodes, fine_owner, fine_parent, mid_owner, mid_parent, neighbours, neighbour_mask,
    up_child_w, up_parent_w, up_out_w, up_bias, up_gain, mid_child_w, mid_parent_w, mid_out_w, mid_bias, mid_gain,
    same_self_w, same_other_w, same_out_w, same_bias, same_gain, down_child_w, down_parent_w, down_out_w,
    down_bias, down_gain,
):
    groups, members = lax.axis_size("grp"), lax.axis_size("dev")
    everyone = groups * members
    fines, width = fine_nodes.shape
    mids, coarses = mid_nodes.shape[0], coarse_nodes.shape[0]
    capacity, mid_capacity = fines // 8, mids // 8
    share = coarses // groups
    everywhere = ("grp", "dev")

    def row(v):
        return v.reshape(1, v.size)

    f_owner, f_parent = row(fine_owner), row(fine_parent)
    m_owner, m_parent = row(mid_owner), row(mid_parent)

    message = shape(capacity + 16, width)
    got = [None] * 4
    for columns in ((0, 3), (1, 2)):
        packed = call(
            pack_fine, [message] * 2, (f_owner, f_parent, fine_nodes), [pltpu.VMEM((capacity, fines), BF16)],
            4 * capacity * fines * width, columns=columns, everyone=everyone, members=members, capacity=capacity,
        )
        for c, p in zip(columns, packed):
            got[c] = from_behind(p, everywhere, OFFSETS[c])

    tile = 512
    flat = pl.BlockSpec((1, tile), lambda i: (0, i))

    def fixed(r, w):
        return pl.BlockSpec((r, w), lambda i: (0, 0))

    own_sum, mid_terms = pl.pallas_call(
        functools.partial(fine_own, everyone=everyone, members=members),
        grid=(fines // tile,),
        out_shape=[shape(mids, width, F32), shape(mids, width)],
        in_specs=[
            flat, flat, pl.BlockSpec((tile, width), lambda i: (i, 0)),
            fixed(mids, width), fixed(width, width), fixed(width, width), fixed(1, width),
        ],
        out_specs=[fixed(mids, width), fixed(mids, width)],
        cost_estimate=pl.CostEstimate(
            flops=2 * width * (fines * (width + 2 * mids) + mids * width), bytes_accessed=6000000, transcendentals=0
        ),
        name="fine_own",
    )(f_owner, f_parent, fine_nodes, mid_nodes, up_parent_w, up_child_w, row(up_bias))

    mid_message = shape(mid_capacity + 16, width)
    mid_update, *packed = call(
        fine_received, [shape(mids, width)] + [mid_message] * 4,
        (*got, mid_terms, own_sum, up_child_w, row(up_bias), up_out_w, row(up_gain), mid_nodes, m_owner, m_parent),
        [pltpu.VMEM((4 * capacity, width), BF16)], 2 * width * (4 * capacity * (width + 2 * mids)),
        members=members, capacity=capacity, mid_capacity=mid_capacity,
    )
    got = [from_behind(p, "dev", o) for p, o in zip(packed, OFFSETS)]

    own_sum, coarse_terms = call(
        mid_own, [shape(coarses, width, F32), shape(coarses, width)],
        (m_owner, m_parent, mid_update, coarse_nodes, mid_parent_w, mid_child_w, row(mid_bias)),
        flops=2 * width * (coarses * width + mids * (width + 2 * coarses)), members=members,
    )
    *shares, labels = call(
        mid_received, [shape(share, width)] * groups + [shape(8, 384, I32)],
        (*got, coarse_terms, own_sum, mid_child_w, row(mid_bias)),
        [pltpu.VMEM((4 * mid_capacity, width), BF16), pltpu.VMEM((coarses, width), F32)],
        2 * width * 4 * mid_capacity * (width + 2 * coarses), groups=groups, capacity=mid_capacity,
    )
    pieces = [shares[0]] + [from_behind(shares[s], "grp", s) for s in range(1, groups)]

    coarse_update, self_terms, other_terms = call(
        coarse_mine, [shape(share, width), shape(share, width, F32), shape(share, width)],
        (*pieces, coarse_nodes, mid_out_w, row(mid_gain), same_self_w, same_other_w, row(same_bias)),
        flops=6 * share * width * width, groups=groups,
    )

    def relayed(value, s):
        pairs = []
        for g in range(groups):
            step = 1 if g + s < groups else -1
            pairs += [(g * members + d, g * members + (d + step) % members) for d in range(members)]
        return lax.ppermute(value, everywhere, pairs)

    same = [from_behind(other_terms, "grp", -s) for s in range(1, groups)]
    low, high = from_behind(other_terms, "dev", 1), from_behind(other_terms, "dev", -1)
    span = -(-(2 * coarses + share) // 128) * 128
    side = [relayed(v, s + 1) for s, v in enumerate(same)]
    (coarse_part,) = call(
        same_level, [shape(share, width)],
        (other_terms, low, high, *same, *side, neighbours, neighbour_mask, self_terms, coarse_update, same_out_w, row(same_gain)),
        [pltpu.VMEM((span, width), BF16)], 2 * width * 6 * share * span, groups=groups, members=members,
    )

    parts = [coarse_part] + [from_behind(coarse_part, "grp", -s) for s in range(1, groups)]
    back = shape(mid_capacity, width)
    coarse_out, *outgoing = call(
        coarse_joined, [shape(coarses, width)] + [back] * 4, (*parts, labels),
        flops=2 * width * 4 * mid_capacity * coarses, groups=groups, capacity=mid_capacity,
    )
    returned = [from_behind(r, "dev", -o) for r, o in zip(outgoing, OFFSETS)]
    (own_terms,) = call(
        down_own, [shape(mids, width, F32)],
        (m_owner, m_parent, coarse_out, mid_update, down_parent_w, down_child_w, row(down_bias)),
        flops=2 * width * mids * (coarses + 2 * width), members=members,
    )
    (mid_out,) = call(
        down_received, [shape(mids, width)],
        (*returned, m_owner, own_terms, mid_update, down_parent_w, down_out_w, row(down_gain)),
        [pltpu.VMEM((4 * mid_capacity, width), BF16)],
        2 * width * mids * (width + 8 * mid_capacity), members=members, capacity=mid_capacity,
    )
    return (mid_out, coarse_out)


def solution(mesh):
    nodes = P(("grp", "dev"), None)
    coarse = P("dev", None)
    flat = P(("grp", "dev"))
    in_specs = (nodes, nodes, coarse, nodes, flat, nodes, flat, coarse, coarse) + (P(),) * 20
    return jax.shard_map(on_device, mesh=mesh, in_specs=in_specs, out_specs=(nodes, coarse), check_vma=False)
```

```python
import functools

import jax
import jax.numpy as jnp
from jax import lax
from jax.experimental import pallas as pl
from jax.experimental.pallas import tpu as pltpu
from jax.sharding import PartitionSpec as P

F32 = jnp.float32
BF16 = jnp.bfloat16
I32 = jnp.int32
VMEM_LIMIT = 24 * 1024 * 1024
OFFSETS = (-2, -1, 1, 2)


def dot(a, b):
    return jnp.dot(a, b, preferred_element_type=F32)


def iota(shape, dim):
    return lax.broadcasted_iota(I32, shape, dim)


def flat_row(x):
    return jnp.concatenate([x[j : j + 1, :] for j in range(x.shape[0])], axis=1)


def one_hot(hit):
    return jnp.where(hit, 1.0, 0.0).astype(BF16)


def columns_of(row):
    return jnp.transpose(jnp.broadcast_to(row, (128, row.shape[1])))


def pick(cols, count):
    lanes = iota(cols.shape, 1)
    return jnp.concatenate([one_hot(cols == lanes + 128 * j) for j in range(count // 128)], axis=1)


def member(row, count):
    return one_hot(iota((count, row.shape[1]), 0) == row)


def silu(v):
    half = 0.5 * v
    return half + half * jnp.tanh(half)


def layer_norm(values, gain):
    center = values - jnp.mean(values, axis=-1, keepdims=True)
    spread = jnp.mean(center * center, axis=-1, keepdims=True)
    return center * lax.rsqrt(spread + 1e-05) * gain


def digits(row):
    high = jnp.floor(row * (1.0 / 256.0))
    low = row - 256.0 * high
    wide = (8, row.shape[1])
    return jnp.concatenate([jnp.broadcast_to(high, wide), jnp.broadcast_to(low, wide)], axis=0).astype(BF16)


def undigits(block):
    values = block.astype(F32)
    return values[0:1] * 256.0 + values[8:9]


def share_at(j, groups):
    half = groups // 2
    g = lax.axis_index("grp")
    own = lax.div(g, half)
    side = own if j < half else 1 - own
    return side * half + lax.rem(lax.rem(g, half) + j % half, half)


def relative_owner(owner, me, total):
    rel = owner - me
    return jnp.where(rel < 0, rel + total, rel)


def places(rel, total, columns, chunk):
    lanes = rel.shape[1]
    subl = iota((8, lanes), 0)
    code = jnp.full((8, lanes), -5, I32)
    for r, c in enumerate(columns):
        code = jnp.where(subl == r, OFFSETS[c] % total, code)
    chosen = jnp.where(rel == code, 1.0, 0.0)
    parts = lanes // chunk
    stacked = jnp.concatenate([chosen[:, chunk * j : chunk * (j + 1)] for j in range(parts)], axis=0)
    below = one_hot(iota((chunk, chunk), 0) < iota((chunk, chunk), 1))
    before = dot(stacked.astype(BF16), below)
    totals = jnp.sum(stacked, axis=1, keepdims=True)
    offset = jnp.zeros((8, 1), F32)
    out = []
    for j in range(parts):
        rows = slice(8 * j, 8 * j + 8)
        out.append(jnp.where(stacked[rows] > 0, before[rows] + offset, -1.0))
        offset = offset + totals[rows]
    return out


def my_index(members):
    return lax.axis_index("grp") * members + lax.axis_index("dev")


def pack_fine(owner, parent, nodes, *rest, columns, everyone, members, capacity):
    outs, picked = rest[: len(columns)], rest[len(columns)]
    rel = relative_owner(owner[...], my_index(members), everyone)
    place = places(rel, everyone, columns, 256)
    label = flat_row(parent[...]).astype(F32) + 1.0
    block = 64
    for r, c in enumerate(columns):
        marks = []
        for i in range(capacity // block):
            slots = (iota((block, 256), 0) + block * i).astype(F32)
            mark = jnp.zeros((block, 128), F32)
            for j, part in enumerate(place):
                hit = jnp.where(part[r : r + 1] == slots, 1.0, 0.0)
                picked[block * i : block * (i + 1), 256 * j : 256 * (j + 1)] = hit.astype(BF16)
                hit = hit * label[:, 256 * j : 256 * (j + 1)]
                mark = mark + hit[:, :128] + hit[:, 128:]
            marks.append(mark)
        spare = jnp.zeros((64, 128), F32)
        marks = [spare] + marks if (capacity * c) % 128 else marks + [spare]
        row = jnp.sum(jnp.transpose(jnp.concatenate(marks, axis=0)), axis=0, keepdims=True)
        outs[r][0:capacity, :] = dot(picked[...], nodes[...]).astype(BF16)
        outs[r][capacity : capacity + 16, 0 : capacity + 64] = digits(row)


def fine_own(owner, parent, nodes, mids, w_parent, w_child, bias, total, terms, *, everyone, members):
    @pl.when(pl.program_id(0) == 0)
    def _():
        terms[...] = dot(mids[...], w_parent[...]).astype(BF16)
        total[...] = jnp.zeros_like(total)

    rel = relative_owner(owner[...], my_index(members), everyone)
    label = jnp.where(rel == 0, flat_row(parent[0]), -1)
    count = terms.shape[0]
    before = dot(nodes[...], w_child[...]) + dot(pick(columns_of(label), count), terms[...]) + bias[...]
    total[...] += dot(member(label, count), silu(before).astype(BF16))


def fine_received(
    m0, m1, m2, m3, terms, own_sum, w_child, bias, w_out, gain, mids, owner, parent,
    update, p0, p1, p2, p3, hidden, *, members, capacity, mid_capacity,
):
    count = terms.shape[0]
    rows = []
    for c, m in enumerate((m0, m1, m2, m3)):
        row = undigits(m[capacity : capacity + 16, 0 : capacity + 64]) - 1.0
        cols = columns_of(row.astype(I32))
        shift = (capacity * c) % 128
        cols = cols[shift : shift + capacity]
        before = dot(m[0:capacity, :], w_child[...]) + dot(pick(cols, count), terms[...]) + bias[...]
        hidden[capacity * c : capacity * (c + 1), :] = silu(before).astype(BF16)
        rows.append(row + 1.0)
    total = own_sum[...]
    for h in range(2):
        a, b = rows[2 * h], rows[2 * h + 1]
        row = jnp.concatenate([a[:, :256], a[:, 256:] + b[:, :128], b[:, 128:]], axis=1) - 1.0
        total = total + dot(member(row.astype(I32), count), hidden[2 * capacity * h : 2 * capacity * (h + 1), :])
    fine_sum = dot(total.astype(BF16), w_out[...])
    new = (mids[...].astype(F32) + layer_norm(fine_sum, gain[...])).astype(BF16)
    update[...] = new
    rel = relative_owner(owner[...], lax.axis_index("dev"), members)
    place = places(rel, members, (0, 1, 2, 3), 128)
    slots = 4 * mid_capacity
    labels = flat_row(parent[...]).astype(F32) + 1.0
    picked, marks = [], jnp.zeros((slots, 128), F32)
    for j, part in enumerate(place):
        base = iota((8, 128), 0).astype(F32) * float(mid_capacity)
        slot = jnp.max(jnp.where(part >= 0, part + base, -1.0), axis=0, keepdims=True)
        hit = slot.astype(I32) == iota((slots, 128), 0)
        picked.append(one_hot(hit))
        marks = marks + jnp.where(hit, labels[:, 128 * j : 128 * (j + 1)], 0.0)
    marks = jnp.concatenate([marks, jnp.zeros((384 - slots, 128), F32)], axis=0)
    code = digits(jnp.sum(jnp.transpose(marks), axis=0, keepdims=True))
    out = dot(jnp.concatenate(picked, axis=1), new).astype(BF16)
    for c, p in enumerate((p0, p1, p2, p3)):
        p[0:mid_capacity, :] = out[mid_capacity * c : mid_capacity * (c + 1)]
        p[mid_capacity : mid_capacity + 16, 0:384] = code


def mid_own(owner, parent, update, coarse, w_parent, w_child, bias, total, terms, *, members):
    terms[...] = dot(coarse[...], w_parent[...]).astype(BF16)
    rel = relative_owner(owner[...], lax.axis_index("dev"), members)
    label = jnp.where(rel == 0, flat_row(parent[...]), -1)
    count = terms.shape[0]
    before = dot(update[...], w_child[...]) + dot(pick(columns_of(label), count), terms[...]) + bias[...]
    total[...] = dot(member(label, count), silu(before).astype(BF16))


def mid_received(m0, m1, m2, m3, terms, own_sum, w_child, bias, *rest, groups, capacity):
    shares, labels, rows, total = rest[:groups], rest[groups], rest[groups + 1], rest[groups + 2]
    count = terms.shape[0]
    lanes = iota((1, 384), 1)
    label = jnp.zeros((1, 384), F32)
    for c, m in enumerate((m0, m1, m2, m3)):
        rows[capacity * c : capacity * (c + 1), :] = m[0:capacity, :]
        row = undigits(m[capacity : capacity + 16, 0:384])
        mine = (lanes >= capacity * c) & (lanes < capacity * (c + 1))
        label = label + jnp.where(mine, row, 0.0)
    label = (label - 1.0).astype(I32)
    labels[...] = jnp.broadcast_to(label, labels.shape)
    slots = 4 * capacity
    cols = columns_of(label)[0:slots]
    before = dot(rows[...], w_child[...]) + dot(pick(cols, count), terms[...]) + bias[...]
    total[...] = own_sum[...] + dot(member(label[:, 0:slots], count), silu(before).astype(BF16))
    share = count // groups
    for j, out in enumerate(shares):
        at = share_at(j, groups) * share
        out[...] = total[pl.ds(pl.multiple_of(at, 16), share), :].astype(BF16)


def coarse_mine(*refs, pieces):
    pieces, refs = refs[:pieces], refs[pieces:]
    coarse, w_out, gain, w_self, w_other, bias, update, own_terms, other = refs
    total = pieces[0][...].astype(F32)
    for p in pieces[1:]:
        total = total + p[...].astype(F32)
    coarse_sum = dot(total.astype(BF16), w_out[...])
    share = update.shape[0]
    at = pl.multiple_of(lax.axis_index("grp") * share, 16)
    new = (coarse[pl.ds(at, share), :].astype(F32) + layer_norm(coarse_sum, gain[...])).astype(BF16)
    update[...] = new
    other[...] = dot(new, w_other[...]).astype(BF16)
    own_terms[...] = dot(new, w_self[...]) + bias[...]


def same_near(*refs, groups, members):
    pieces = refs[:groups]
    low, high, near, mask, found, far_ids, used, window, turned = refs[groups:]
    share = pieces[0].shape[0]
    half, count = groups // 2, groups * share
    part = half * share
    for j, piece in enumerate(pieces):
        at = part + share_at(j, groups) * share
        window[pl.ds(pl.multiple_of(at, 16), share), :] = piece[...]
    g, d = lax.axis_index("grp"), lax.axis_index("dev")
    side = lax.div(g, half)
    for j in range(half):
        at = pl.multiple_of((share_at(j, groups) - side * half) * share, 16)
        rows = slice(share * j, share * (j + 1))
        window[pl.ds(at, share), :] = low[rows, :]
        window[pl.ds(part + count + at, share), :] = high[rows, :]
    own = pl.ds(pl.multiple_of(g * share, 8), share)
    slots = near.shape[0]
    pad = jnp.zeros((128 - slots, count), I32)
    turned[...] = jnp.transpose(jnp.concatenate([mask[...], pad], axis=0))
    used[...] = turned[own, :].astype(F32)
    turned[...] = jnp.transpose(jnp.concatenate([near[...], pad], axis=0))
    whole = members * count
    rel = turned[own, :] - (d - 1) * count
    rel = jnp.where(rel < 0, rel + whole, rel)
    rel = jnp.where(rel >= whole, rel - whole, rel)
    shift = side * part
    place = jnp.where(rel < count, rel - shift, jnp.where(rel < 2 * count, rel - part, rel - shift - part))
    lost = ((rel < count) & ((place < 0) | (place >= part))) | ((rel >= 2 * count) & ((place < part + count) | (place >= 2 * count)))
    place = jnp.where(lost, -1, place)
    far_ids[...] = rel - jnp.where(side == 0, part, 2 * count)
    for k in range(slots):
        cols = jnp.broadcast_to(place[:, k : k + 1], (share, 128))
        found[share * k : share * (k + 1), :] = dot(pick(cols, window.shape[0]), window[...])


def same_far(*refs, groups, slots):
    far, found, far_ids, used, own_terms, update, w_out, gain, result, window = refs
    share = result.shape[0]
    half = groups // 2
    side = lax.div(lax.axis_index("grp"), half)
    for j in range(half):
        at = pl.multiple_of((share_at(j, groups) - side * half) * share, 16)
        window[pl.ds(at, share), :] = far[share * j : share * (j + 1), :]
    hidden = jnp.zeros((share, result.shape[1]), F32)
    for k in range(slots):
        cols = jnp.broadcast_to(far_ids[:, k : k + 1], (share, 128))
        got = found[share * k : share * (k + 1), :] + dot(pick(cols, window.shape[0]), window[...])
        h = silu(own_terms[...] + got).astype(BF16).astype(F32)
        hidden = hidden + used[:, k : k + 1] * h
    same_sum = dot(hidden.astype(BF16), w_out[...])
    result[...] = (update[...].astype(F32) + layer_norm(same_sum, gain[...])).astype(BF16)


def coarse_joined(*refs, groups, capacity):
    pieces = refs[:groups]
    labels, result, r0, r1, r2, r3 = refs[groups:]
    share = pieces[0].shape[0]
    for j, p in enumerate(pieces):
        at = share_at(j, groups) * share
        result[pl.ds(pl.multiple_of(at, 16), share), :] = p[...]
    cols = columns_of(labels[0:1, :])[0 : 4 * capacity]
    rows = dot(pick(cols, result.shape[0]), result[...]).astype(BF16)
    for c, r in enumerate((r0, r1, r2, r3)):
        r[...] = rows[capacity * c : capacity * (c + 1)]


def down_own(owner, parent, coarse, update, w_parent, w_child, bias, result, *, members):
    rel = relative_owner(owner[...], lax.axis_index("dev"), members)
    label = jnp.where(rel == 0, flat_row(parent[...]), -1)
    rows = dot(pick(columns_of(label), coarse.shape[0]), coarse[...]).astype(BF16)
    terms = dot(rows, w_parent[...]).astype(BF16).astype(F32)
    result[...] = dot(update[...], w_child[...]) + terms + bias[...]


def down_received(r0, r1, r2, r3, owner, own_terms, update, w_parent, w_out, gain, result, rows, *, members, capacity):
    for c, r in enumerate((r0, r1, r2, r3)):
        rows[capacity * c : capacity * (c + 1), :] = r[...]
    slots = 4 * capacity
    terms = dot(rows[...], w_parent[...]).astype(BF16)
    rel = relative_owner(owner[...], lax.axis_index("dev"), members)
    place = places(rel, members, (0, 1, 2, 3), 128)
    back = []
    for part in place:
        base = iota((8, 128), 0).astype(F32) * float(capacity)
        slot = jnp.max(jnp.where(part >= 0, part + base, -1.0), axis=0, keepdims=True)
        cols = columns_of(slot.astype(I32))
        wide = jnp.concatenate([cols, cols, cols], axis=1)[:, 0:slots]
        back.append(one_hot(wide == iota((128, slots), 1)))
    before = own_terms[...] + dot(jnp.concatenate(back, axis=0), terms)
    messages = dot(silu(before).astype(BF16), w_out[...])
    result[...] = (update[...].astype(F32) + layer_norm(messages, gain[...])).astype(BF16)


def shape(rows, width, kind=BF16):
    return jax.ShapeDtypeStruct((rows, width), kind)


def call(body, outs, args, scratch=(), flops=0, name=None, **static):
    moved = sum(a.size * a.dtype.itemsize for a in (*args, *outs))
    return pl.pallas_call(
        functools.partial(body, **static),
        out_shape=outs,
        in_specs=[pl.BlockSpec(memory_space=pltpu.VMEM)] * len(args),
        out_specs=[pl.BlockSpec(memory_space=pltpu.VMEM)] * len(outs),
        scratch_shapes=list(scratch),
        cost_estimate=pl.CostEstimate(flops=flops, bytes_accessed=moved, transcendentals=0),
        compiler_params=pltpu.CompilerParams(vmem_limit_bytes=VMEM_LIMIT),
        name=name or body.__name__,
    )(*args)


def from_behind(value, axis, steps):
    count = lax.axis_size(axis)
    return lax.ppermute(value, axis, [(s, (s + steps) % count) for s in range(count)])


def on_device(
    fine_nodes, mid_nodes, coarse_nodes, fine_owner, fine_parent, mid_owner, mid_parent, neighbours, neighbour_mask,
    up_child_w, up_parent_w, up_out_w, up_bias, up_gain, mid_child_w, mid_parent_w, mid_out_w, mid_bias, mid_gain,
    same_self_w, same_other_w, same_out_w, same_bias, same_gain, down_child_w, down_parent_w, down_out_w,
    down_bias, down_gain,
):
    groups, members = lax.axis_size("grp"), lax.axis_size("dev")
    everyone = groups * members
    fines, width = fine_nodes.shape
    mids, coarses = mid_nodes.shape[0], coarse_nodes.shape[0]
    capacity, mid_capacity = fines // 8, mids // 8
    share = coarses // groups
    everywhere = ("grp", "dev")

    def row(v):
        return v.reshape(1, v.size)

    f_owner, f_parent = row(fine_owner), fine_parent.reshape(-1, 128)
    m_owner, m_parent = row(mid_owner), mid_parent.reshape(-1, 128)
    half = groups // 2

    def moved(value, source):
        return lax.ppermute(value, "grp", [(source(g // half, g % half), g) for g in range(groups)])

    def across(value):
        return moved(value, lambda h, y: (1 - h) * half + y)

    def around(value, s):
        return moved(value, lambda h, y: h * half + (y + s) % half)

    def gathered(value):
        other = across(value)
        near = [around(value, s) for s in range(1, half)]
        return [value, *near, other] + [around(other, s) for s in range(1, half)]

    message = shape(capacity + 16, width)
    got = [None] * 4
    for columns in ((0, 3), (1, 2)):
        packed = call(
            pack_fine, [message] * 2, (f_owner, f_parent, fine_nodes), [pltpu.VMEM((capacity, fines), BF16)],
            4 * capacity * fines * width, columns=columns, everyone=everyone, members=members, capacity=capacity,
        )
        for c, p in zip(columns, packed):
            got[c] = from_behind(p, everywhere, OFFSETS[c])

    tile = 512
    flat = pl.BlockSpec((1, tile), lambda i: (0, i))

    def fixed(r, w):
        return pl.BlockSpec((r, w), lambda i: (0, 0))

    own_sum, mid_terms = pl.pallas_call(
        functools.partial(fine_own, everyone=everyone, members=members),
        grid=(fines // tile,),
        out_shape=[shape(mids, width, F32), shape(mids, width)],
        in_specs=[
            flat, pl.BlockSpec((1, tile // 128, 128), lambda i: (i, 0, 0)), pl.BlockSpec((tile, width), lambda i: (i, 0)),
            fixed(mids, width), fixed(width, width), fixed(width, width), fixed(1, width),
        ],
        out_specs=[fixed(mids, width), fixed(mids, width)],
        cost_estimate=pl.CostEstimate(
            flops=2 * width * (fines * (width + 2 * mids) + mids * width), bytes_accessed=6000000, transcendentals=0
        ),
        compiler_params=pltpu.CompilerParams(vmem_limit_bytes=VMEM_LIMIT),
        name="fine_own",
    )(f_owner, fine_parent.reshape(-1, tile // 128, 128), fine_nodes, mid_nodes, up_parent_w, up_child_w, row(up_bias))

    mid_message = shape(mid_capacity + 16, width)
    mid_update, *packed = call(
        fine_received, [shape(mids, width)] + [mid_message] * 4,
        (*got, mid_terms, own_sum, up_child_w, row(up_bias), up_out_w, row(up_gain), mid_nodes, m_owner, m_parent),
        [pltpu.VMEM((4 * capacity, width), BF16)], 2 * width * (4 * capacity * (width + 2 * mids)),
        members=members, capacity=capacity, mid_capacity=mid_capacity,
    )
    got = [from_behind(p, "dev", o) for p, o in zip(packed, OFFSETS)]

    own_sum, coarse_terms = call(
        mid_own, [shape(coarses, width, F32), shape(coarses, width)],
        (m_owner, m_parent, mid_update, coarse_nodes, mid_parent_w, mid_child_w, row(mid_bias)),
        flops=2 * width * (coarses * width + mids * (width + 2 * coarses)), members=members,
    )
    *shares, labels = call(
        mid_received, [shape(share, width)] * groups + [shape(8, 384, I32)],
        (*got, coarse_terms, own_sum, mid_child_w, row(mid_bias)),
        [pltpu.VMEM((4 * mid_capacity, width), BF16), pltpu.VMEM((coarses, width), F32)],
        2 * width * 4 * mid_capacity * (width + 2 * coarses), groups=groups, capacity=mid_capacity,
    )
    first = [around(shares[half + s], -s) for s in range(1, half)]
    second = [around(shares[s], -s) for s in range(1, half)]
    total = sum(p.astype(F32) for p in (shares[half], *first)).astype(BF16)
    pieces = [shares[0], *second, across(total)]

    coarse_update, self_terms, other_terms = call(
        coarse_mine, [shape(share, width), shape(share, width, F32), shape(share, width)],
        (*pieces, coarse_nodes, mid_out_w, row(mid_gain), same_self_w, same_other_w, row(same_bias)),
        flops=6 * share * width * width, pieces=len(pieces),
    )

    same = gathered(other_terms)
    near_half = jnp.concatenate(same[:half], axis=0)
    far_half = jnp.concatenate(same[half:], axis=0)
    low, high = from_behind(near_half, "dev", 1), from_behind(near_half, "dev", -1)
    pairs = []
    for g in range(groups):
        step = 1 if g < half else -1
        pairs += [(g * members + d, g * members + (d + step) % members) for d in range(members)]
    far = lax.ppermute(far_half, everywhere, pairs)
    slots = neighbours.shape[1]
    found, far_ids, used = call(
        same_near, [shape(slots * share, width, F32), shape(share, 128, I32), shape(share, 128, F32)],
        (*same, low, high, neighbours.T, neighbour_mask.T),
        [pltpu.VMEM((2 * coarses, width), BF16), pltpu.VMEM((coarses, 128), I32)],
        2 * width * slots * share * 2 * coarses, groups=groups, members=members,
    )
    (coarse_part,) = call(
        same_far, [shape(share, width)],
        (far, found, far_ids, used, self_terms, coarse_update, same_out_w, row(same_gain)),
        [pltpu.VMEM((coarses // 2, width), BF16)], width * slots * share * coarses, groups=groups, slots=slots,
    )

    parts = gathered(coarse_part)
    back = shape(mid_capacity, width)
    coarse_out, *outgoing = call(
        coarse_joined, [shape(coarses, width)] + [back] * 4, (*parts, labels),
        flops=2 * width * 4 * mid_capacity * coarses, groups=groups, capacity=mid_capacity,
    )
    returned = [from_behind(r, "dev", -o) for r, o in zip(outgoing, OFFSETS)]
    (own_terms,) = call(
        down_own, [shape(mids, width, F32)],
        (m_owner, m_parent, coarse_out, mid_update, down_parent_w, down_child_w, row(down_bias)),
        flops=2 * width * mids * (coarses + 2 * width), members=members,
    )
    (mid_out,) = call(
        down_received, [shape(mids, width)],
        (*returned, m_owner, own_terms, mid_update, down_parent_w, down_out_w, row(down_gain)),
        [pltpu.VMEM((4 * mid_capacity, width), BF16)],
        2 * width * mids * (width + 8 * mid_capacity), members=members, capacity=mid_capacity,
    )
    return (mid_out, coarse_out)


def solution(mesh):
    nodes = P(("grp", "dev"), None)
    coarse = P("dev", None)
    flat = P(("grp", "dev"))
    in_specs = (nodes, nodes, coarse, nodes, flat, nodes, flat, coarse, coarse) + (P(),) * 20
    return jax.shard_map(on_device, mesh=mesh, in_specs=in_specs, out_specs=(nodes, coarse), check_vma=False)
```

```python
import functools

import jax
import jax.numpy as jnp
from jax import lax
from jax.experimental import pallas as pl
from jax.experimental.pallas import tpu as pltpu
from jax.sharding import PartitionSpec as P

F32 = jnp.float32
BF16 = jnp.bfloat16
I32 = jnp.int32
VMEM_LIMIT = 24 * 1024 * 1024
OFFSETS = (-2, -1, 1, 2)


def dot(a, b):
    return jnp.dot(a, b, preferred_element_type=F32)


def iota(shape, dim):
    return lax.broadcasted_iota(I32, shape, dim)


def flat_row(x):
    return jnp.concatenate([x[j : j + 1, :] for j in range(x.shape[0])], axis=1)


def one_hot(hit):
    return jnp.where(hit, 1.0, 0.0).astype(BF16)


def columns_of(row):
    return jnp.transpose(jnp.broadcast_to(row, (128, row.shape[1])))


def pick(cols, count):
    lanes = iota(cols.shape, 1)
    return jnp.concatenate([one_hot(cols == lanes + 128 * j) for j in range(count // 128)], axis=1)


def member(row, count):
    return one_hot(iota((count, row.shape[1]), 0) == row)


def silu(v):
    half = 0.5 * v
    return half + half * jnp.tanh(half)


def layer_norm(values, gain):
    center = values - jnp.mean(values, axis=-1, keepdims=True)
    spread = jnp.mean(center * center, axis=-1, keepdims=True)
    return center * lax.rsqrt(spread + 1e-05) * gain


def digits(row):
    high = jnp.floor(row * (1.0 / 256.0))
    low = row - 256.0 * high
    wide = (8, row.shape[1])
    return jnp.concatenate([jnp.broadcast_to(high, wide), jnp.broadcast_to(low, wide)], axis=0).astype(BF16)


def undigits(block):
    values = block.astype(F32)
    return values[0:1] * 256.0 + values[8:9]


def share_at(j, groups):
    half = groups // 2
    g = lax.axis_index("grp")
    own = lax.div(g, half)
    side = own if j < half else 1 - own
    return side * half + lax.rem(lax.rem(g, half) + j % half, half)


def relative_owner(owner, me, total):
    rel = owner - me
    return jnp.where(rel < 0, rel + total, rel)


def places(rel, total, columns, chunk):
    lanes = rel.shape[1]
    subl = iota((8, lanes), 0)
    code = jnp.full((8, lanes), -5, I32)
    for r, c in enumerate(columns):
        code = jnp.where(subl == r, OFFSETS[c] % total, code)
    chosen = jnp.where(rel == code, 1.0, 0.0)
    parts = lanes // chunk
    stacked = jnp.concatenate([chosen[:, chunk * j : chunk * (j + 1)] for j in range(parts)], axis=0)
    below = one_hot(iota((chunk, chunk), 0) < iota((chunk, chunk), 1))
    before = dot(stacked.astype(BF16), below)
    totals = jnp.sum(stacked, axis=1, keepdims=True)
    offset = jnp.zeros((8, 1), F32)
    out = []
    for j in range(parts):
        rows = slice(8 * j, 8 * j + 8)
        out.append(jnp.where(stacked[rows] > 0, before[rows] + offset, -1.0))
        offset = offset + totals[rows]
    return out


def my_index(members):
    return lax.axis_index("grp") * members + lax.axis_index("dev")


def start_copies(pairs, sems):
    copies = [pltpu.make_async_copy(a, b, sems.at[i]) for i, (a, b) in enumerate(pairs)]
    for c in copies:
        c.start()
    return copies


def packed_rows(place, label, nodes, out, c, capacity):
    block, chunk = 64, 512
    marks = [jnp.zeros((block, 128), F32) for _ in range(capacity // block)]
    total = None
    for j in range(place.shape[1] // chunk):
        lanes = slice(chunk * j, chunk * (j + 1))
        rows = []
        for i in range(capacity // block):
            slots = (iota((block, chunk), 0) + block * i).astype(F32)
            hit = jnp.where(place[:, lanes] == slots, 1.0, 0.0)
            rows.append(hit.astype(BF16))
            hit = hit * label[:, lanes]
            marks[i] = marks[i] + ((hit[:, :128] + hit[:, 128:256]) + (hit[:, 256:384] + hit[:, 384:]))
        part = dot(jnp.concatenate(rows, axis=0), nodes[lanes, :])
        total = part if total is None else total + part
    spare = [jnp.zeros((64, 128), F32)]
    marks = spare + marks if (capacity * c) % 128 else marks + spare
    row = jnp.sum(jnp.transpose(jnp.concatenate(marks, axis=0)), axis=0, keepdims=True)
    out[0:capacity, :] = total.astype(BF16)
    out[capacity : capacity + 16, 0 : capacity + 64] = digits(row)


def pack_first(owner_in, parent_in, nodes_in, m0, m1, nodes, place, label, owner, parent, sems, *, columns, everyone, members, capacity):
    copies = start_copies([(owner_in, owner), (parent_in, parent), (nodes_in, nodes)], sems)
    copies[0].wait()
    copies[1].wait()
    rel = relative_owner(owner[...], my_index(members), everyone)
    for j, part in enumerate(places(rel, everyone, (0, 1, 2, 3), 256)):
        place[:, 256 * j : 256 * (j + 1)] = part
    target = flat_row(parent[...]).astype(F32)
    label[0:1, :] = target + 1.0
    label[1:2, :] = jnp.where(rel == 0, target, -1.0)
    copies[2].wait()
    for c, out in zip(columns, (m0, m1)):
        packed_rows(place[c : c + 1, :], label[0:1, :], nodes, out, c, capacity)


def pack_second(place, label, nodes, a_in, b_in, c_in, m0, m1, a, b, c, sems, *, columns, capacity):
    copies = start_copies([(a_in, a), (b_in, b), (c_in, c)], sems)
    for at, out in zip(columns, (m0, m1)):
        packed_rows(place[at : at + 1, :], label[0:1, :], nodes, out, at, capacity)
    for copy in copies:
        copy.wait()


def fine_own(labels, nodes, mids, w_parent, w_child, bias, total, terms, *, tile):
    terms[...] = dot(mids[...], w_parent[...]).astype(BF16)
    count = terms.shape[0]
    total[...] = jnp.zeros_like(total)

    def step(i, _):
        at = pl.multiple_of(i * tile, tile)
        label = labels[1:2, pl.ds(at, tile)].astype(I32)
        before = dot(nodes[pl.ds(at, tile), :], w_child[...]) + dot(pick(columns_of(label), count), terms[...]) + bias[...]
        total[...] += dot(member(label, count), silu(before).astype(BF16))
        return 0

    lax.fori_loop(0, nodes.shape[0] // tile, step, 0)


def fine_received(
    m0, m1, m2, m3, terms, own_sum, w_child, bias, w_out, gain, mids, owner, parent,
    update, p0, p1, p2, p3, slot_row, hidden, *, members, capacity, mid_capacity,
):
    count = terms.shape[0]
    rows = []
    for c, m in enumerate((m0, m1, m2, m3)):
        row = undigits(m[capacity : capacity + 16, 0 : capacity + 64]) - 1.0
        cols = columns_of(row.astype(I32))
        shift = (capacity * c) % 128
        cols = cols[shift : shift + capacity]
        before = dot(m[0:capacity, :], w_child[...]) + dot(pick(cols, count), terms[...]) + bias[...]
        hidden[capacity * c : capacity * (c + 1), :] = silu(before).astype(BF16)
        rows.append(row + 1.0)
    label = []
    for a, b in (rows[0:2], rows[2:4]):
        label += [a[:, :256], a[:, 256:] + b[:, :128], b[:, 128:]]
    label = jnp.concatenate(label, axis=1) - 1.0
    total = own_sum[...] + dot(member(label.astype(I32), count), hidden[...])
    fine_sum = dot(total.astype(BF16), w_out[...])
    new = (mids[...].astype(F32) + layer_norm(fine_sum, gain[...])).astype(BF16)
    update[...] = new
    rel = relative_owner(owner[...], lax.axis_index("dev"), members)
    place = places(rel, members, (0, 1, 2, 3), 128)
    slots = 4 * mid_capacity
    labels = flat_row(parent[...]).astype(F32) + 1.0
    picked, marks = [], jnp.zeros((slots, 128), F32)
    for j, part in enumerate(place):
        base = iota((8, 128), 0).astype(F32) * float(mid_capacity)
        slot = jnp.max(jnp.where(part >= 0, part + base, -1.0), axis=0, keepdims=True)
        slot_row[:, 128 * j : 128 * (j + 1)] = jnp.broadcast_to(slot.astype(I32), (8, 128))
        hit = jnp.where(slot == iota((slots, 128), 0).astype(F32), 1.0, 0.0)
        picked.append(hit.astype(BF16))
        marks = marks + hit * labels[:, 128 * j : 128 * (j + 1)]
    marks = jnp.concatenate([marks, jnp.zeros((384 - slots, 128), F32)], axis=0)
    code = digits(jnp.sum(jnp.transpose(marks), axis=0, keepdims=True))
    out = dot(jnp.concatenate(picked, axis=1), new).astype(BF16)
    for c, p in enumerate((p0, p1, p2, p3)):
        p[0:mid_capacity, :] = out[mid_capacity * c : mid_capacity * (c + 1)]
        p[mid_capacity : mid_capacity + 16, 0:384] = code


def mid_own(owner, parent, update, coarse, w_parent, w_child, bias, total, terms, *, members):
    terms[...] = dot(coarse[...], w_parent[...]).astype(BF16)
    rel = relative_owner(owner[...], lax.axis_index("dev"), members)
    label = jnp.where(rel == 0, flat_row(parent[...]), -1)
    count = terms.shape[0]
    before = dot(update[...], w_child[...]) + dot(pick(columns_of(label), count), terms[...]) + bias[...]
    total[...] = dot(member(label, count), silu(before).astype(BF16))


def mid_received(m0, m1, m2, m3, terms, own_sum, w_child, bias, *rest, groups, capacity):
    shares, labels, rows, total = rest[:groups], rest[groups], rest[groups + 1], rest[groups + 2]
    count = terms.shape[0]
    lanes = iota((1, 384), 1)
    label = jnp.zeros((1, 384), F32)
    for c, m in enumerate((m0, m1, m2, m3)):
        rows[capacity * c : capacity * (c + 1), :] = m[0:capacity, :]
        row = undigits(m[capacity : capacity + 16, 0:384])
        mine = (lanes >= capacity * c) & (lanes < capacity * (c + 1))
        label = label + jnp.where(mine, row, 0.0)
    label = (label - 1.0).astype(I32)
    labels[...] = jnp.broadcast_to(label, labels.shape)
    slots = 4 * capacity
    cols = columns_of(label)[0:slots]
    before = dot(rows[...], w_child[...]) + dot(pick(cols, count), terms[...]) + bias[...]
    total[...] = own_sum[...] + dot(member(label[:, 0:slots], count), silu(before).astype(BF16))
    share = count // groups
    for j, out in enumerate(shares):
        at = share_at(j, groups) * share
        out[...] = total[pl.ds(pl.multiple_of(at, 16), share), :].astype(BF16)


def coarse_mine(*refs, pieces):
    pieces, refs = refs[:pieces], refs[pieces:]
    coarse, w_out, gain, w_self, w_other, bias, update, own_terms, other = refs
    total = pieces[0][...].astype(F32)
    for p in pieces[1:]:
        total = total + p[...].astype(F32)
    coarse_sum = dot(total.astype(BF16), w_out[...])
    share = update.shape[0]
    at = pl.multiple_of(lax.axis_index("grp") * share, 16)
    new = (coarse[pl.ds(at, share), :].astype(F32) + layer_norm(coarse_sum, gain[...])).astype(BF16)
    update[...] = new
    other[...] = dot(new, w_other[...]).astype(BF16)
    own_terms[...] = dot(new, w_self[...]) + bias[...]


def same_near(*refs, groups, members):
    pieces = refs[:groups]
    low, high, near, mask, found, far_ids, used, window, turned = refs[groups:]
    share = pieces[0].shape[0]
    half, count = groups // 2, groups * share
    part = half * share
    for j, piece in enumerate(pieces):
        at = part + share_at(j, groups) * share
        window[pl.ds(pl.multiple_of(at, 16), share), :] = piece[...]
    g, d = lax.axis_index("grp"), lax.axis_index("dev")
    side = lax.div(g, half)
    for j in range(half):
        at = pl.multiple_of((share_at(j, groups) - side * half) * share, 16)
        rows = slice(share * j, share * (j + 1))
        window[pl.ds(at, share), :] = low[rows, :]
        window[pl.ds(part + count + at, share), :] = high[rows, :]
    own = pl.ds(pl.multiple_of(g * share, 8), share)
    slots = near.shape[0]
    pad = jnp.zeros((128 - slots, count), I32)
    turned[...] = jnp.transpose(jnp.concatenate([mask[...], pad], axis=0))
    used[...] = turned[own, :].astype(F32)
    turned[...] = jnp.transpose(jnp.concatenate([near[...], pad], axis=0))
    whole = members * count
    rel = turned[own, :] - (d - 1) * count
    rel = jnp.where(rel < 0, rel + whole, rel)
    rel = jnp.where(rel >= whole, rel - whole, rel)
    shift = side * part
    place = jnp.where(rel < count, rel - shift, jnp.where(rel < 2 * count, rel - part, rel - shift - part))
    lost = ((rel < count) & ((place < 0) | (place >= part))) | ((rel >= 2 * count) & ((place < part + count) | (place >= 2 * count)))
    place = jnp.where(lost, -1, place)
    far_ids[...] = rel - jnp.where(side == 0, part, 2 * count)
    for k in range(slots):
        cols = jnp.broadcast_to(place[:, k : k + 1], (share, 128))
        found[share * k : share * (k + 1), :] = dot(pick(cols, window.shape[0]), window[...])


def same_far(*refs, groups, slots):
    far, found, far_ids, used, own_terms, update, w_out, gain, result, window = refs
    share = result.shape[0]
    half = groups // 2
    side = lax.div(lax.axis_index("grp"), half)
    for j in range(half):
        at = pl.multiple_of((share_at(j, groups) - side * half) * share, 16)
        window[pl.ds(at, share), :] = far[share * j : share * (j + 1), :]
    hidden = jnp.zeros((share, result.shape[1]), F32)
    for k in range(slots):
        cols = jnp.broadcast_to(far_ids[:, k : k + 1], (share, 128))
        got = found[share * k : share * (k + 1), :] + dot(pick(cols, window.shape[0]), window[...])
        h = silu(own_terms[...] + got).astype(BF16).astype(F32)
        hidden = hidden + used[:, k : k + 1] * h
    same_sum = dot(hidden.astype(BF16), w_out[...])
    result[...] = (update[...].astype(F32) + layer_norm(same_sum, gain[...])).astype(BF16)


def coarse_joined(*refs, groups, capacity):
    pieces = refs[:groups]
    labels, result, kept, r0, r1, r2, r3 = refs[groups:]
    share = pieces[0].shape[0]
    for j, p in enumerate(pieces):
        at = share_at(j, groups) * share
        kept[pl.ds(pl.multiple_of(at, 16), share), :] = p[...]
    result[...] = kept[...]
    cols = columns_of(labels[0:1, :])[0 : 4 * capacity]
    rows = dot(pick(cols, kept.shape[0]), kept[...]).astype(BF16)
    for c, r in enumerate((r0, r1, r2, r3)):
        r[...] = rows[capacity * c : capacity * (c + 1)]


def down_ready(owner, parent, slot_row, update, w_child, bias, after, child_terms, own_rows, back, *, coarses, slots, members):
    rel = relative_owner(owner[...], lax.axis_index("dev"), members)
    label = jnp.where(rel == 0, flat_row(parent[...]), -1)
    own_rows[...] = pick(columns_of(label), coarses)
    back[...] = pick(columns_of(slot_row[0:1, :]), back.shape[1])
    child_terms[...] = dot(update[...], w_child[...]) + bias[...]


def down_own(own_rows, coarse, w_parent, child_terms, result):
    rows = dot(own_rows[...], coarse[...]).astype(BF16)
    terms = dot(rows, w_parent[...]).astype(BF16).astype(F32)
    result[...] = child_terms[...] + terms


def down_received(r0, r1, r2, r3, back, own_terms, update, w_parent, w_out, gain, result, rows, *, capacity):
    for c, r in enumerate((r0, r1, r2, r3)):
        rows[capacity * c : capacity * (c + 1), :] = r[...]
    slots = 4 * capacity
    terms = dot(rows[...], w_parent[...]).astype(BF16)
    before = own_terms[...] + dot(back[:, 0:slots], terms)
    messages = dot(silu(before).astype(BF16), w_out[...])
    result[...] = (update[...].astype(F32) + layer_norm(messages, gain[...])).astype(BF16)


def shape(rows, width, kind=BF16):
    return jax.ShapeDtypeStruct((rows, width), kind)


def call(body, outs, args, scratch=(), flops=0, name=None, outside=(), **static):
    moved = sum(a.size * a.dtype.itemsize for a in (*args, *outs))
    return pl.pallas_call(
        functools.partial(body, **static),
        out_shape=outs,
        in_specs=[
            pl.BlockSpec(memory_space=pltpu.HBM if i in outside else pltpu.VMEM) for i in range(len(args))
        ],
        out_specs=[pl.BlockSpec(memory_space=pltpu.VMEM)] * len(outs),
        scratch_shapes=list(scratch),
        cost_estimate=pl.CostEstimate(flops=flops, bytes_accessed=moved, transcendentals=0),
        compiler_params=pltpu.CompilerParams(vmem_limit_bytes=VMEM_LIMIT),
        name=name or body.__name__,
    )(*[pltpu.with_memory_space_constraint(a, pltpu.HBM) if i in outside else a for i, a in enumerate(args)])


def from_behind(value, axis, steps):
    count = lax.axis_size(axis)
    return lax.ppermute(value, axis, [(s, (s + steps) % count) for s in range(count)])


def on_device(
    fine_nodes, mid_nodes, coarse_nodes, fine_owner, fine_parent, mid_owner, mid_parent, neighbours, neighbour_mask,
    up_child_w, up_parent_w, up_out_w, up_bias, up_gain, mid_child_w, mid_parent_w, mid_out_w, mid_bias, mid_gain,
    same_self_w, same_other_w, same_out_w, same_bias, same_gain, down_child_w, down_parent_w, down_out_w,
    down_bias, down_gain,
):
    groups, members = lax.axis_size("grp"), lax.axis_size("dev")
    everyone = groups * members
    fines, width = fine_nodes.shape
    mids, coarses = mid_nodes.shape[0], coarse_nodes.shape[0]
    capacity, mid_capacity = fines // 8, mids // 8
    share = coarses // groups
    everywhere = ("grp", "dev")

    def row(v):
        return v.reshape(1, v.size)

    f_owner, f_parent = row(fine_owner), fine_parent.reshape(-1, 128)
    m_owner, m_parent = row(mid_owner), mid_parent.reshape(-1, 128)
    half = groups // 2

    def moved(value, source):
        return lax.ppermute(value, "grp", [(source(g // half, g % half), g) for g in range(groups)])

    def across(value):
        return moved(value, lambda h, y: (1 - h) * half + y)

    def around(value, s):
        return moved(value, lambda h, y: h * half + (y + s) % half)

    def gathered(value):
        other = across(value)
        near = [around(value, s) for s in range(1, half)]
        return [value, *near, other] + [around(other, s) for s in range(1, half)]

    message = shape(capacity + 16, width)
    got = [None] * 4
    work = 4 * capacity * fines * width
    m0, m1, nodes, place, label = call(
        pack_first, [message] * 2 + [shape(fines, width), shape(8, fines, F32), shape(8, fines, F32)],
        (f_owner, f_parent, fine_nodes),
        [pltpu.VMEM(f_owner.shape, I32), pltpu.VMEM(f_parent.shape, I32), pltpu.SemaphoreType.DMA((3,))],
        work, outside=(0, 1, 2), columns=(0, 3), everyone=everyone, members=members, capacity=capacity,
    )
    got[0], got[3] = from_behind(m0, everywhere, OFFSETS[0]), from_behind(m1, everywhere, OFFSETS[3])
    m0, m1, mid_copy, w_parent, w_child = call(
        pack_second, [message] * 2 + [shape(mids, width)] + [shape(width, width)] * 2,
        (place, label, nodes, mid_nodes, up_parent_w, up_child_w), [pltpu.SemaphoreType.DMA((3,))],
        work, outside=(3, 4, 5), columns=(1, 2), capacity=capacity,
    )
    got[1], got[2] = from_behind(m0, everywhere, OFFSETS[1]), from_behind(m1, everywhere, OFFSETS[2])
    own_sum, mid_terms = call(
        fine_own, [shape(mids, width, F32), shape(mids, width)],
        (label, nodes, mid_copy, w_parent, w_child, row(up_bias)),
        flops=2 * width * (fines * (width + 2 * mids) + mids * width), tile=512,
    )

    mid_message = shape(mid_capacity + 16, width)
    mid_update, *packed, slot_row = call(
        fine_received, [shape(mids, width)] + [mid_message] * 4 + [shape(8, mids, I32)],
        (*got, mid_terms, own_sum, w_child, row(up_bias), up_out_w, row(up_gain), mid_copy, m_owner, m_parent),
        [pltpu.VMEM((4 * capacity, width), BF16)], 2 * width * (4 * capacity * (width + 2 * mids)),
        members=members, capacity=capacity, mid_capacity=mid_capacity,
    )
    got = [from_behind(p, "dev", o) for p, o in zip(packed, OFFSETS)]

    own_sum, coarse_terms = call(
        mid_own, [shape(coarses, width, F32), shape(coarses, width)],
        (m_owner, m_parent, mid_update, coarse_nodes, mid_parent_w, mid_child_w, row(mid_bias)),
        flops=2 * width * (coarses * width + mids * (width + 2 * coarses)), members=members,
    )
    *shares, labels = call(
        mid_received, [shape(share, width)] * groups + [shape(8, 384, I32)],
        (*got, coarse_terms, own_sum, mid_child_w, row(mid_bias)),
        [pltpu.VMEM((4 * mid_capacity, width), BF16), pltpu.VMEM((coarses, width), F32)],
        2 * width * 4 * mid_capacity * (width + 2 * coarses), groups=groups, capacity=mid_capacity,
    )
    first = [around(shares[half + s], -s) for s in range(1, half)]
    second = [around(shares[s], -s) for s in range(1, half)]
    total = sum(p.astype(F32) for p in (shares[half], *first)).astype(BF16)
    pieces = [shares[0], *second, across(total)]

    coarse_update, self_terms, other_terms = call(
        coarse_mine, [shape(share, width), shape(share, width, F32), shape(share, width)],
        (*pieces, coarse_nodes, mid_out_w, row(mid_gain), same_self_w, same_other_w, row(same_bias)),
        flops=6 * share * width * width, pieces=len(pieces),
    )

    same = gathered(other_terms)
    near_half = jnp.concatenate(same[:half], axis=0)
    far_half = jnp.concatenate(same[half:], axis=0)
    low, high = from_behind(near_half, "dev", 1), from_behind(near_half, "dev", -1)
    pairs = []
    for g in range(groups):
        step = 1 if g < half else -1
        pairs += [(g * members + d, g * members + (d + step) % members) for d in range(members)]
    far = lax.ppermute(far_half, everywhere, pairs)
    slots = neighbours.shape[1]
    found, far_ids, used = call(
        same_near, [shape(slots * share, width, F32), shape(share, 128, I32), shape(share, 128, F32)],
        (*same, low, high, neighbours.T, neighbour_mask.T),
        [pltpu.VMEM((2 * coarses, width), BF16), pltpu.VMEM((coarses, 128), I32)],
        2 * width * slots * share * 2 * coarses, groups=groups, members=members,
    )
    (coarse_part,) = call(
        same_far, [shape(share, width)],
        (far, found, far_ids, used, self_terms, coarse_update, same_out_w, row(same_gain)),
        [pltpu.VMEM((coarses // 2, width), BF16)], width * slots * share * coarses, groups=groups, slots=slots,
    )

    parts = gathered(coarse_part)
    mid_slots = 4 * mid_capacity
    child_terms, own_rows, back = call(
        down_ready, [shape(mids, width, F32), shape(mids, coarses), shape(mids, -(-mid_slots // 128) * 128)],
        (m_owner, m_parent, slot_row, mid_update, down_child_w, row(down_bias), other_terms),
        flops=2 * width * mids * width, coarses=coarses, slots=mid_slots, members=members,
    )
    piece = shape(mid_capacity, width)
    coarse_out, kept, *outgoing = call(
        coarse_joined, [shape(coarses, width)] * 2 + [piece] * 4, (*parts, labels),
        flops=2 * width * mid_slots * coarses, groups=groups, capacity=mid_capacity,
    )
    returned = [from_behind(r, "dev", -o) for r, o in zip(outgoing, OFFSETS)]
    (own_terms,) = call(
        down_own, [shape(mids, width, F32)], (own_rows, kept, down_parent_w, child_terms),
        flops=2 * width * mids * (coarses + width),
    )
    (mid_out,) = call(
        down_received, [shape(mids, width)],
        (*returned, back, own_terms, mid_update, down_parent_w, down_out_w, row(down_gain)),
        [pltpu.VMEM((mid_slots, width), BF16)], 2 * width * mids * (width + 2 * mid_slots), capacity=mid_capacity,
    )
    return (mid_out, coarse_out)


def solution(mesh):
    nodes = P(("grp", "dev"), None)
    coarse = P("dev", None)
    flat = P(("grp", "dev"))
    in_specs = (nodes, nodes, coarse, nodes, flat, nodes, flat, coarse, coarse) + (P(),) * 20
    return jax.shard_map(on_device, mesh=mesh, in_specs=in_specs, out_specs=(nodes, coarse), check_vma=False)
```

```python
import functools

import jax
import jax.numpy as jnp
from jax import lax
from jax.experimental import pallas as pl
from jax.experimental.pallas import tpu as pltpu
from jax.sharding import PartitionSpec as P

F32 = jnp.float32
BF16 = jnp.bfloat16
I32 = jnp.int32
VMEM_LIMIT = 24 * 1024 * 1024


def dot(a, b):
    return jnp.dot(a, b, preferred_element_type=F32)


def iota(shape, dim):
    return lax.broadcasted_iota(I32, shape, dim)


def flat_row(x):
    return jnp.concatenate([x[j : j + 1, :] for j in range(x.shape[0])], axis=1)


def one_hot(hit):
    return jnp.where(hit, 1.0, 0.0).astype(BF16)


def columns_of(row):
    return jnp.transpose(jnp.broadcast_to(row, (128, row.shape[1])))


def pick(cols, count):
    lanes = iota(cols.shape, 1)
    return jnp.concatenate([one_hot(cols == lanes + 128 * j) for j in range(count // 128)], axis=1)


def member(row, count):
    return one_hot(iota((count, row.shape[1]), 0) == row)


def silu(v):
    half = 0.5 * v
    return half + half * jnp.tanh(half)


def layer_norm(values, gain):
    center = values - jnp.mean(values, axis=-1, keepdims=True)
    spread = jnp.mean(center * center, axis=-1, keepdims=True)
    return center * lax.rsqrt(spread + 1e-05) * gain


def digits(row):
    high = jnp.floor(row * (1.0 / 256.0))
    low = row - 256.0 * high
    wide = (8, row.shape[1])
    return jnp.concatenate([jnp.broadcast_to(high, wide), jnp.broadcast_to(low, wide)], axis=0).astype(BF16)


def undigits(block):
    values = block.astype(F32)
    return values[0:1] * 256.0 + values[8:9]


def share_at(j, groups):
    half = groups // 2
    g = lax.axis_index("grp")
    own = lax.div(g, half)
    side = own if j < half else 1 - own
    return side * half + lax.rem(lax.rem(g, half) + j % half, half)


def relative_owner(owner, me, total):
    rel = owner - me
    return jnp.where(rel < 0, rel + total, rel)


def places(rel, total, columns, chunk):
    lanes = rel.shape[1]
    subl = iota((8, lanes), 0)
    code = jnp.full((8, lanes), -5, I32)
    side = 1 - 2 * lax.rem(lax.axis_index("dev"), 2)
    steps = (-2, side, -side, 2)
    for r, c in enumerate(columns):
        code = jnp.where(subl == r, lax.rem(steps[c] + total, total), code)
    chosen = jnp.where(rel == code, 1.0, 0.0)
    parts = lanes // chunk
    stacked = jnp.concatenate([chosen[:, chunk * j : chunk * (j + 1)] for j in range(parts)], axis=0)
    below = one_hot(iota((chunk, chunk), 0) < iota((chunk, chunk), 1))
    before = dot(stacked.astype(BF16), below)
    totals = jnp.sum(stacked, axis=1, keepdims=True)
    offset = jnp.zeros((8, 1), F32)
    out = []
    for j in range(parts):
        rows = slice(8 * j, 8 * j + 8)
        out.append(jnp.where(stacked[rows] > 0, before[rows] + offset, -1.0))
        offset = offset + totals[rows]
    return out


def my_index(members):
    return lax.axis_index("grp") * members + lax.axis_index("dev")


def start_copies(pairs, sems):
    copies = [pltpu.make_async_copy(a, b, sems.at[i]) for i, (a, b) in enumerate(pairs)]
    for c in copies:
        c.start()
    return copies


def packed_rows(place, label, nodes, out, c, capacity, chunk, waits=()):
    block = 64
    marks = [jnp.zeros((block, 128), F32) for _ in range(capacity // block)]
    total = None
    for j in range(place.shape[1] // chunk):
        lanes = slice(chunk * j, chunk * (j + 1))
        rows = []
        for i in range(capacity // block):
            slots = (iota((block, chunk), 0) + block * i).astype(F32)
            hit = jnp.where(place[:, lanes] == slots, 1.0, 0.0)
            rows.append(hit.astype(BF16))
            hit = hit * label[:, lanes]
            marks[i] = marks[i] + ((hit[:, :128] + hit[:, 128:256]) + (hit[:, 256:384] + hit[:, 384:]))
        if waits:
            waits[j].wait()
        part = dot(jnp.concatenate(rows, axis=0), nodes[lanes, :])
        total = part if total is None else total + part
    spare = [jnp.zeros((64, 128), F32)]
    marks = spare + marks if (capacity * c) % 128 else marks + spare
    row = jnp.sum(jnp.transpose(jnp.concatenate(marks, axis=0)), axis=0, keepdims=True)
    out[0:capacity, :] = total.astype(BF16)
    out[capacity : capacity + 16, 0 : capacity + 64] = digits(row)


def pack_first(owner_in, parent_in, nodes_in, m0, m1, nodes, place, label, owner, parent, sems, *, columns, everyone, members, capacity):
    chunk = 512
    parts = [pl.ds(chunk * j, chunk) for j in range(nodes.shape[0] // chunk)]
    copies = start_copies([(owner_in, owner), (parent_in, parent), *[(nodes_in.at[p], nodes.at[p]) for p in parts]], sems)
    copies[0].wait()
    copies[1].wait()
    rel = relative_owner(owner[...], my_index(members), everyone)
    for j, part in enumerate(places(rel, everyone, (0, 1, 2, 3), 256)):
        place[:, 256 * j : 256 * (j + 1)] = part
    target = flat_row(parent[...]).astype(F32)
    label[0:1, :] = target + 1.0
    label[1:2, :] = jnp.where(rel == 0, target, -1.0)
    for c, out, waits in zip(columns, (m0, m1), (copies[2:], ())):
        packed_rows(place[c : c + 1, :], label[0:1, :], nodes, out, c, capacity, chunk, waits)


def pack_second(place, label, nodes, a_in, b_in, c_in, m0, m1, a, b, c, sems, *, columns, capacity):
    copies = start_copies([(a_in, a), (b_in, b), (c_in, c)], sems)
    for at, out in zip(columns, (m0, m1)):
        packed_rows(place[at : at + 1, :], label[0:1, :], nodes, out, at, capacity, 512)
    for copy in copies:
        copy.wait()


def fine_own(labels, nodes, mids, w_parent, w_child, bias, total, terms, *, tile):
    terms[...] = dot(mids[...], w_parent[...]).astype(BF16)
    count = terms.shape[0]
    total[...] = jnp.zeros_like(total)

    def step(i, _):
        at = pl.multiple_of(i * tile, tile)
        label = labels[1:2, pl.ds(at, tile)].astype(I32)
        before = dot(nodes[pl.ds(at, tile), :], w_child[...]) + dot(pick(columns_of(label), count), terms[...]) + bias[...]
        total[...] += dot(member(label, count), silu(before).astype(BF16))
        return 0

    lax.fori_loop(0, nodes.shape[0] // tile, step, 0)


def fine_received(
    m0, m1, m2, m3, terms, own_sum, w_child, bias, w_out, gain, mids, owner, parent,
    update, p0, p1, p2, p3, slot_row, hidden, *, members, capacity, mid_capacity,
):
    count = terms.shape[0]
    rows = []
    for c, m in enumerate((m0, m1, m2, m3)):
        row = undigits(m[capacity : capacity + 16, 0 : capacity + 64]) - 1.0
        cols = columns_of(row.astype(I32))
        shift = (capacity * c) % 128
        cols = cols[shift : shift + capacity]
        before = dot(m[0:capacity, :], w_child[...]) + dot(pick(cols, count), terms[...]) + bias[...]
        hidden[capacity * c : capacity * (c + 1), :] = silu(before).astype(BF16)
        rows.append(row + 1.0)
    label = []
    for a, b in (rows[0:2], rows[2:4]):
        label += [a[:, :256], a[:, 256:] + b[:, :128], b[:, 128:]]
    label = jnp.concatenate(label, axis=1) - 1.0
    total = own_sum[...] + dot(member(label.astype(I32), count), hidden[...])
    fine_sum = dot(total.astype(BF16), w_out[...])
    new = (mids[...].astype(F32) + layer_norm(fine_sum, gain[...])).astype(BF16)
    update[...] = new
    rel = relative_owner(owner[...], lax.axis_index("dev"), members)
    place = places(rel, members, (0, 1, 2, 3), 128)
    slots = 4 * mid_capacity
    labels = flat_row(parent[...]).astype(F32) + 1.0
    picked, marks = [], jnp.zeros((slots, 128), F32)
    for j, part in enumerate(place):
        base = iota((8, 128), 0).astype(F32) * float(mid_capacity)
        slot = jnp.max(jnp.where(part >= 0, part + base, -1.0), axis=0, keepdims=True)
        slot_row[:, 128 * j : 128 * (j + 1)] = jnp.broadcast_to(slot.astype(I32), (8, 128))
        hit = jnp.where(slot == iota((slots, 128), 0).astype(F32), 1.0, 0.0)
        picked.append(hit.astype(BF16))
        marks = marks + hit * labels[:, 128 * j : 128 * (j + 1)]
    marks = jnp.concatenate([marks, jnp.zeros((384 - slots, 128), F32)], axis=0)
    code = digits(jnp.sum(jnp.transpose(marks), axis=0, keepdims=True))
    out = dot(jnp.concatenate(picked, axis=1), new).astype(BF16)
    for c, p in enumerate((p0, p1, p2, p3)):
        p[0:mid_capacity, :] = out[mid_capacity * c : mid_capacity * (c + 1)]
        p[mid_capacity : mid_capacity + 16, 0:384] = code


def mid_own(owner, parent, update, coarse, w_parent, w_child, bias, total, terms, *, members):
    terms[...] = dot(coarse[...], w_parent[...]).astype(BF16)
    rel = relative_owner(owner[...], lax.axis_index("dev"), members)
    label = jnp.where(rel == 0, flat_row(parent[...]), -1)
    count = terms.shape[0]
    before = dot(update[...], w_child[...]) + dot(pick(columns_of(label), count), terms[...]) + bias[...]
    total[...] = dot(member(label, count), silu(before).astype(BF16))


def mid_received(m0, m1, m2, m3, terms, own_sum, w_child, bias, *rest, groups, capacity):
    shares, labels, rows, total = rest[:groups], rest[groups], rest[groups + 1], rest[groups + 2]
    count = terms.shape[0]
    lanes = iota((1, 384), 1)
    label = jnp.zeros((1, 384), F32)
    for c, m in enumerate((m0, m1, m2, m3)):
        rows[capacity * c : capacity * (c + 1), :] = m[0:capacity, :]
        row = undigits(m[capacity : capacity + 16, 0:384])
        mine = (lanes >= capacity * c) & (lanes < capacity * (c + 1))
        label = label + jnp.where(mine, row, 0.0)
    label = (label - 1.0).astype(I32)
    labels[...] = jnp.broadcast_to(label, labels.shape)
    slots = 4 * capacity
    cols = columns_of(label)[0:slots]
    before = dot(rows[...], w_child[...]) + dot(pick(cols, count), terms[...]) + bias[...]
    total[...] = own_sum[...] + dot(member(label[:, 0:slots], count), silu(before).astype(BF16))
    share = count // groups
    for j, out in enumerate(shares):
        at = share_at(j, groups) * share
        out[...] = total[pl.ds(pl.multiple_of(at, 16), share), :].astype(BF16)


def coarse_mine(*refs, pieces):
    pieces, refs = refs[:pieces], refs[pieces:]
    coarse, w_out, gain, w_self, w_other, bias, update, own_terms, other = refs
    total = pieces[0][...].astype(F32)
    for p in pieces[1:]:
        total = total + p[...].astype(F32)
    coarse_sum = dot(total.astype(BF16), w_out[...])
    share = update.shape[0]
    at = pl.multiple_of(lax.axis_index("grp") * share, 16)
    new = (coarse[pl.ds(at, share), :].astype(F32) + layer_norm(coarse_sum, gain[...])).astype(BF16)
    update[...] = new
    other[...] = dot(new, w_other[...]).astype(BF16)
    own_terms[...] = dot(new, w_self[...]) + bias[...]


def same_near(*refs, groups, members):
    pieces = refs[:groups]
    low, high, near, mask, found, far_ids, used, window, turned = refs[groups:]
    share = pieces[0].shape[0]
    half, count = groups // 2, groups * share
    part = half * share
    for j, piece in enumerate(pieces):
        at = part + share_at(j, groups) * share
        window[pl.ds(pl.multiple_of(at, 16), share), :] = piece[...]
    g, d = lax.axis_index("grp"), lax.axis_index("dev")
    side = lax.div(g, half)
    for j in range(half):
        at = pl.multiple_of((share_at(j, groups) - side * half) * share, 16)
        rows = slice(share * j, share * (j + 1))
        window[pl.ds(at, share), :] = low[rows, :]
        window[pl.ds(part + count + at, share), :] = high[rows, :]
    own = pl.ds(pl.multiple_of(g * share, 8), share)
    slots = near.shape[0]
    pad = jnp.zeros((128 - slots, count), I32)
    turned[...] = jnp.transpose(jnp.concatenate([mask[...], pad], axis=0))
    used[...] = turned[own, :].astype(F32)
    turned[...] = jnp.transpose(jnp.concatenate([near[...], pad], axis=0))
    whole = members * count
    rel = turned[own, :] - (d - 1) * count
    rel = jnp.where(rel < 0, rel + whole, rel)
    rel = jnp.where(rel >= whole, rel - whole, rel)
    shift = side * part
    place = jnp.where(rel < count, rel - shift, jnp.where(rel < 2 * count, rel - part, rel - shift - part))
    lost = ((rel < count) & ((place < 0) | (place >= part))) | ((rel >= 2 * count) & ((place < part + count) | (place >= 2 * count)))
    place = jnp.where(lost, -1, place)
    far_ids[...] = rel - jnp.where(side == 0, part, 2 * count)
    for k in range(slots):
        cols = jnp.broadcast_to(place[:, k : k + 1], (share, 128))
        found[share * k : share * (k + 1), :] = dot(pick(cols, window.shape[0]), window[...])


def same_far(*refs, groups, slots):
    far, found, far_ids, used, own_terms, update, w_out, gain, result, window = refs
    share = result.shape[0]
    half = groups // 2
    side = lax.div(lax.axis_index("grp"), half)
    for j in range(half):
        at = pl.multiple_of((share_at(j, groups) - side * half) * share, 16)
        window[pl.ds(at, share), :] = far[share * j : share * (j + 1), :]
    hidden = jnp.zeros((share, result.shape[1]), F32)
    for k in range(slots):
        cols = jnp.broadcast_to(far_ids[:, k : k + 1], (share, 128))
        got = found[share * k : share * (k + 1), :] + dot(pick(cols, window.shape[0]), window[...])
        h = silu(own_terms[...] + got).astype(BF16).astype(F32)
        hidden = hidden + used[:, k : k + 1] * h
    same_sum = dot(hidden.astype(BF16), w_out[...])
    result[...] = (update[...].astype(F32) + layer_norm(same_sum, gain[...])).astype(BF16)


def coarse_joined(*refs, groups, capacity):
    pieces = refs[:groups]
    labels, kept, r0, r1, r2, r3 = refs[groups:]
    share = pieces[0].shape[0]
    for j, p in enumerate(pieces):
        at = share_at(j, groups) * share
        kept[pl.ds(pl.multiple_of(at, 16), share), :] = p[...]
    cols = columns_of(labels[0:1, :])[0 : 4 * capacity]
    rows = dot(pick(cols, kept.shape[0]), kept[...]).astype(BF16)
    for c, r in enumerate((r0, r1, r2, r3)):
        r[...] = rows[capacity * c : capacity * (c + 1)]


def down_ready(owner, parent, slot_row, update, w_child, bias, after, child_terms, own_rows, back, *, coarses, slots, members):
    rel = relative_owner(owner[...], lax.axis_index("dev"), members)
    label = jnp.where(rel == 0, flat_row(parent[...]), -1)
    own_rows[...] = pick(columns_of(label), coarses)
    back[...] = pick(columns_of(slot_row[0:1, :]), back.shape[1])
    child_terms[...] = dot(update[...], w_child[...]) + bias[...]


def down_own(own_rows, coarse, w_parent, child_terms, result, whole):
    whole[...] = coarse[...]
    rows = dot(own_rows[...], coarse[...]).astype(BF16)
    terms = dot(rows, w_parent[...]).astype(BF16).astype(F32)
    result[...] = child_terms[...] + terms


def down_received(r0, r1, r2, r3, back, own_terms, update, w_parent, w_out, gain, result, rows, *, capacity):
    for c, r in enumerate((r0, r1, r2, r3)):
        rows[capacity * c : capacity * (c + 1), :] = r[...]
    slots = 4 * capacity
    terms = dot(rows[...], w_parent[...]).astype(BF16)
    before = own_terms[...] + dot(back[:, 0:slots], terms)
    messages = dot(silu(before).astype(BF16), w_out[...])
    result[...] = (update[...].astype(F32) + layer_norm(messages, gain[...])).astype(BF16)


def shape(rows, width, kind=BF16):
    return jax.ShapeDtypeStruct((rows, width), kind)


def call(body, outs, args, scratch=(), flops=0, name=None, outside=(), **static):
    moved = sum(a.size * a.dtype.itemsize for a in (*args, *outs))
    return pl.pallas_call(
        functools.partial(body, **static),
        out_shape=outs,
        in_specs=[
            pl.BlockSpec(memory_space=pltpu.HBM if i in outside else pltpu.VMEM) for i in range(len(args))
        ],
        out_specs=[pl.BlockSpec(memory_space=pltpu.VMEM)] * len(outs),
        scratch_shapes=list(scratch),
        cost_estimate=pl.CostEstimate(flops=flops, bytes_accessed=moved, transcendentals=0),
        compiler_params=pltpu.CompilerParams(vmem_limit_bytes=VMEM_LIMIT),
        name=name or body.__name__,
    )(*[pltpu.with_memory_space_constraint(a, pltpu.HBM) if i in outside else a for i, a in enumerate(args)])


def from_behind(value, axis, steps):
    count = lax.axis_size(axis)
    return lax.ppermute(value, axis, [(s, (s + steps) % count) for s in range(count)])


def spilled(value, axis, c, back=False):
    count = lax.axis_size(axis)
    step = -2 if (c == 0) != back else 2
    pairs = []
    for s in range(count):
        target = (s + step, s ^ 1, s + 1 if s % 2 else s - 1, s + step)[c]
        pairs.append((s, target % count))
    return lax.ppermute(value, axis, pairs)


def on_device(
    fine_nodes, mid_nodes, coarse_nodes, fine_owner, fine_parent, mid_owner, mid_parent, neighbours, neighbour_mask,
    up_child_w, up_parent_w, up_out_w, up_bias, up_gain, mid_child_w, mid_parent_w, mid_out_w, mid_bias, mid_gain,
    same_self_w, same_other_w, same_out_w, same_bias, same_gain, down_child_w, down_parent_w, down_out_w,
    down_bias, down_gain,
):
    groups, members = lax.axis_size("grp"), lax.axis_size("dev")
    everyone = groups * members
    fines, width = fine_nodes.shape
    mids, coarses = mid_nodes.shape[0], coarse_nodes.shape[0]
    capacity, mid_capacity = fines // 8, mids // 8
    share = coarses // groups
    everywhere = ("grp", "dev")

    def row(v):
        return v.reshape(1, v.size)

    f_owner, f_parent = row(fine_owner), fine_parent.reshape(-1, 128)
    m_owner, m_parent = row(mid_owner), mid_parent.reshape(-1, 128)
    half = groups // 2

    def moved(value, source):
        return lax.ppermute(value, "grp", [(source(g // half, g % half), g) for g in range(groups)])

    def across(value):
        return moved(value, lambda h, y: (1 - h) * half + y)

    def around(value, s):
        return moved(value, lambda h, y: h * half + (y + s) % half)

    def gathered(value):
        other = across(value)
        near = [around(value, s) for s in range(1, half)]
        return [value, *near, other] + [around(other, s) for s in range(1, half)]

    message = shape(capacity + 16, width)
    work = 4 * capacity * fines * width
    first, second = (0, 3), (2, 1)
    m0, m1, nodes, place, label = call(
        pack_first, [message] * 2 + [shape(fines, width), shape(8, fines, F32), shape(8, fines, F32)],
        (f_owner, f_parent, fine_nodes),
        [pltpu.VMEM(f_owner.shape, I32), pltpu.VMEM(f_parent.shape, I32), pltpu.SemaphoreType.DMA((2 + fines // 512,))],
        work, outside=(0, 1, 2), columns=first, everyone=everyone, members=members, capacity=capacity,
    )
    got = {c: spilled(m, everywhere, c) for m, c in zip((m0, m1), first)}
    m0, m1, mid_copy, w_parent, w_child = call(
        pack_second, [message] * 2 + [shape(mids, width)] + [shape(width, width)] * 2,
        (place, label, nodes, mid_nodes, up_parent_w, up_child_w), [pltpu.SemaphoreType.DMA((3,))],
        work, outside=(3, 4, 5), columns=second, capacity=capacity,
    )
    got |= {c: spilled(m, everywhere, c) for m, c in zip((m0, m1), second)}
    own_sum, mid_terms = call(
        fine_own, [shape(mids, width, F32), shape(mids, width)],
        (label, nodes, mid_copy, w_parent, w_child, row(up_bias)),
        flops=2 * width * (fines * (width + 2 * mids) + mids * width), tile=1280,
    )

    mid_message = shape(mid_capacity + 16, width)
    mid_update, *packed, slot_row = call(
        fine_received, [shape(mids, width)] + [mid_message] * 4 + [shape(8, mids, I32)],
        (*[got[c] for c in range(4)], mid_terms, own_sum, w_child, row(up_bias), up_out_w, row(up_gain), mid_copy, m_owner, m_parent),
        [pltpu.VMEM((4 * capacity, width), BF16)], 2 * width * (4 * capacity * (width + 2 * mids)),
        members=members, capacity=capacity, mid_capacity=mid_capacity,
    )
    got = [spilled(p, "dev", c) for c, p in enumerate(packed)]

    own_sum, coarse_terms = call(
        mid_own, [shape(coarses, width, F32), shape(coarses, width)],
        (m_owner, m_parent, mid_update, coarse_nodes, mid_parent_w, mid_child_w, row(mid_bias)),
        flops=2 * width * (coarses * width + mids * (width + 2 * coarses)), members=members,
    )
    *shares, labels = call(
        mid_received, [shape(share, width)] * groups + [shape(8, 384, I32)],
        (*got, coarse_terms, own_sum, mid_child_w, row(mid_bias)),
        [pltpu.VMEM((4 * mid_capacity, width), BF16), pltpu.VMEM((coarses, width), F32)],
        2 * width * 4 * mid_capacity * (width + 2 * coarses), groups=groups, capacity=mid_capacity,
    )
    first = [around(shares[half + s], -s) for s in range(1, half)]
    second = [around(shares[s], -s) for s in range(1, half)]
    total = sum(p.astype(F32) for p in (shares[half], *first)).astype(BF16)
    pieces = [shares[0], *second, across(total)]

    coarse_update, self_terms, other_terms = call(
        coarse_mine, [shape(share, width), shape(share, width, F32), shape(share, width)],
        (*pieces, coarse_nodes, mid_out_w, row(mid_gain), same_self_w, same_other_w, row(same_bias)),
        flops=6 * share * width * width, pieces=len(pieces),
    )

    same = gathered(other_terms)
    near_half = jnp.concatenate(same[:half], axis=0)
    far_half = jnp.concatenate(same[half:], axis=0)
    low, high = from_behind(near_half, "dev", 1), from_behind(near_half, "dev", -1)
    pairs = []
    for g in range(groups):
        step = 1 if g < half else -1
        pairs += [(g * members + d, g * members + (d + step) % members) for d in range(members)]
    far = lax.ppermute(far_half, everywhere, pairs)
    slots = neighbours.shape[1]
    found, far_ids, used = call(
        same_near, [shape(slots * share, width, F32), shape(share, 128, I32), shape(share, 128, F32)],
        (*same, low, high, neighbours.T, neighbour_mask.T),
        [pltpu.VMEM((2 * coarses, width), BF16), pltpu.VMEM((coarses, 128), I32)],
        2 * width * slots * share * 2 * coarses, groups=groups, members=members,
    )
    (coarse_part,) = call(
        same_far, [shape(share, width)],
        (far, found, far_ids, used, self_terms, coarse_update, same_out_w, row(same_gain)),
        [pltpu.VMEM((coarses // 2, width), BF16)], width * slots * share * coarses, groups=groups, slots=slots,
    )

    parts = gathered(coarse_part)
    mid_slots = 4 * mid_capacity
    child_terms, own_rows, back = call(
        down_ready, [shape(mids, width, F32), shape(mids, coarses), shape(mids, -(-mid_slots // 128) * 128)],
        (m_owner, m_parent, slot_row, mid_update, down_child_w, row(down_bias), other_terms),
        flops=2 * width * mids * width, coarses=coarses, slots=mid_slots, members=members,
    )
    piece = shape(mid_capacity, width)
    kept, *outgoing = call(
        coarse_joined, [shape(coarses, width)] + [piece] * 4, (*parts, labels),
        flops=2 * width * mid_slots * coarses, groups=groups, capacity=mid_capacity,
    )
    returned = [spilled(r, "dev", c, back=True) for c, r in enumerate(outgoing)]
    own_terms, coarse_out = call(
        down_own, [shape(mids, width, F32), shape(coarses, width)], (own_rows, kept, down_parent_w, child_terms),
        flops=2 * width * mids * (coarses + width),
    )
    (mid_out,) = call(
        down_received, [shape(mids, width)],
        (*returned, back, own_terms, mid_update, down_parent_w, down_out_w, row(down_gain)),
        [pltpu.VMEM((mid_slots, width), BF16)], 2 * width * mids * (width + 2 * mid_slots), capacity=mid_capacity,
    )
    return (mid_out, coarse_out)


def solution(mesh):
    nodes = P(("grp", "dev"), None)
    coarse = P("dev", None)
    flat = P(("grp", "dev"))
    in_specs = (nodes, nodes, coarse, nodes, flat, nodes, flat, coarse, coarse) + (P(),) * 20
    return jax.shard_map(on_device, mesh=mesh, in_specs=in_specs, out_specs=(nodes, coarse), check_vma=False)
```

```python
import functools

import jax
import jax.numpy as jnp
from jax import lax
from jax.experimental import pallas as pl
from jax.experimental.pallas import tpu as pltpu
from jax.sharding import PartitionSpec as P


F32 = jnp.float32
BF16 = jnp.bfloat16
I32 = jnp.int32
VMEM_LIMIT = 24 * 1024 * 1024


def dot(a, b):
    return jnp.dot(a, b, preferred_element_type=F32)


def iota(shape, dim):
    return lax.broadcasted_iota(I32, shape, dim)


def flat_row(x):
    return jnp.concatenate([x[j : j + 1, :] for j in range(x.shape[0])], axis=1)


def one_hot(hit):
    return jnp.where(hit, 1.0, 0.0).astype(BF16)


def columns_of(row):
    return jnp.transpose(jnp.broadcast_to(row, (128, row.shape[1])))


def pick(cols, count):
    lanes = iota(cols.shape, 1)
    return jnp.concatenate([one_hot(cols == lanes + 128 * j) for j in range(count // 128)], axis=1)


def member(row, count):
    return one_hot(iota((count, row.shape[1]), 0) == row)


def silu(v):
    half = 0.5 * v
    return half + half * jnp.tanh(half)


def layer_norm(values, gain):
    center = values - jnp.mean(values, axis=-1, keepdims=True)
    spread = jnp.mean(center * center, axis=-1, keepdims=True)
    return center * lax.rsqrt(spread + 1e-05) * gain


def digits(row):
    high = jnp.floor(row * (1.0 / 256.0))
    low = row - 256.0 * high
    wide = (8, row.shape[1])
    return jnp.concatenate([jnp.broadcast_to(high, wide), jnp.broadcast_to(low, wide)], axis=0).astype(BF16)


def undigits(block):
    values = block.astype(F32)
    return values[0:1] * 256.0 + values[8:9]


def share_at(j, groups):
    half = groups // 2
    g = lax.axis_index("grp")
    own = lax.div(g, half)
    side = own if j < half else 1 - own
    return side * half + lax.rem(lax.rem(g, half) + j % half, half)


def relative_owner(owner, me, total):
    rel = owner - me
    return jnp.where(rel < 0, rel + total, rel)


def places(rel, total, columns, chunk):
    lanes = rel.shape[1]
    subl = iota((8, lanes), 0)
    code = jnp.full((8, lanes), -5, I32)
    side = 1 - 2 * lax.rem(lax.axis_index("dev"), 2)
    steps = (-2, side, -side, 2)
    for r, c in enumerate(columns):
        code = jnp.where(subl == r, lax.rem(steps[c] + total, total), code)
    chosen = jnp.where(rel == code, 1.0, 0.0)
    parts = lanes // chunk
    stacked = jnp.concatenate([chosen[:, chunk * j : chunk * (j + 1)] for j in range(parts)], axis=0)
    below = one_hot(iota((chunk, chunk), 0) < iota((chunk, chunk), 1))
    before = dot(stacked.astype(BF16), below)
    totals = jnp.sum(stacked, axis=1, keepdims=True)
    offset = jnp.zeros((8, 1), F32)
    out = []
    for j in range(parts):
        rows = slice(8 * j, 8 * j + 8)
        out.append(jnp.where(stacked[rows] > 0, before[rows] + offset, -1.0))
        offset = offset + totals[rows]
    return out


def my_index(members):
    return lax.axis_index("grp") * members + lax.axis_index("dev")


def start_copies(pairs, sems):
    copies = [pltpu.make_async_copy(a, b, sems.at[i]) for i, (a, b) in enumerate(pairs)]
    for c in copies:
        c.start()
    return copies


def packed_rows(place, label, nodes, out, c, capacity, chunk, waits=()):
    block = 64
    marks = [jnp.zeros((block, 128), F32) for _ in range(capacity // block)]
    total = None
    for j in range(place.shape[1] // chunk):
        lanes = slice(chunk * j, chunk * (j + 1))
        rows = []
        for i in range(capacity // block):
            slots = (iota((block, chunk), 0) + block * i).astype(F32)
            hit = jnp.where(place[:, lanes] == slots, 1.0, 0.0)
            rows.append(hit.astype(BF16))
            hit = hit * label[:, lanes]
            marks[i] = marks[i] + ((hit[:, :128] + hit[:, 128:256]) + (hit[:, 256:384] + hit[:, 384:]))
        if waits:
            waits[j].wait()
        part = dot(jnp.concatenate(rows, axis=0), nodes[lanes, :])
        total = part if total is None else total + part
    spare = [jnp.zeros((64, 128), F32)]
    marks = spare + marks if (capacity * c) % 128 else marks + spare
    row = jnp.sum(jnp.transpose(jnp.concatenate(marks, axis=0)), axis=0, keepdims=True)
    out[0:capacity, :] = total.astype(BF16)
    out[capacity : capacity + 16, 0 : capacity + 64] = digits(row)


def pack_first(owner_in, parent_in, nodes_in, out, nodes, place, label, owner, parent, sems, *, column, everyone, members, capacity):
    chunk = 512
    parts = [pl.ds(chunk * j, chunk) for j in range(nodes.shape[0] // chunk)]
    copies = start_copies([(owner_in, owner), (parent_in, parent), *[(nodes_in.at[p], nodes.at[p]) for p in parts]], sems)
    copies[0].wait()
    copies[1].wait()
    rel = relative_owner(owner[...], my_index(members), everyone)
    for j, part in enumerate(places(rel, everyone, (0, 1, 2, 3), 256)):
        place[:, 256 * j : 256 * (j + 1)] = part
    target = flat_row(parent[...]).astype(F32)
    label[0:1, :] = target + 1.0
    label[1:2, :] = jnp.where(rel == 0, target, -1.0)
    packed_rows(place[column : column + 1, :], label[0:1, :], nodes, out, column, capacity, chunk, copies[2:])


def pack_next(place, label, nodes, *rest, column, capacity):
    count = (len(rest) - 1) // 2
    copies = start_copies(list(zip(rest[:count], rest[count + 1 :])), rest[-1]) if count else []
    packed_rows(place[column : column + 1, :], label[0:1, :], nodes, rest[count], column, capacity, 512)
    for copy in copies:
        copy.wait()


def fine_own(labels, nodes, mids, w_parent, w_child, bias, total, terms, *, tile):
    terms[...] = dot(mids[...], w_parent[...]).astype(BF16)
    count = terms.shape[0]
    total[...] = jnp.zeros_like(total)

    def step(i, _):
        at = pl.multiple_of(i * tile, tile)
        label = labels[1:2, pl.ds(at, tile)].astype(I32)
        before = dot(nodes[pl.ds(at, tile), :], w_child[...]) + dot(pick(columns_of(label), count), terms[...]) + bias[...]
        total[...] += dot(member(label, count), silu(before).astype(BF16))
        return 0

    lax.fori_loop(0, nodes.shape[0] // tile, step, 0)


def fine_received(
    m0, m1, m2, m3, terms, own_sum, w_child, bias, w_out, gain, mids, owner, parent,
    update, p0, p1, p2, p3, slot_row, hidden, *, members, capacity, mid_capacity,
):
    count = terms.shape[0]
    rows = []
    for c, m in enumerate((m0, m1, m2, m3)):
        row = undigits(m[capacity : capacity + 16, 0 : capacity + 64]) - 1.0
        cols = columns_of(row.astype(I32))
        shift = (capacity * c) % 128
        cols = cols[shift : shift + capacity]
        before = dot(m[0:capacity, :], w_child[...]) + dot(pick(cols, count), terms[...]) + bias[...]
        hidden[capacity * c : capacity * (c + 1), :] = silu(before).astype(BF16)
        rows.append(row + 1.0)
    label = []
    for a, b in (rows[0:2], rows[2:4]):
        label += [a[:, :256], a[:, 256:] + b[:, :128], b[:, 128:]]
    label = jnp.concatenate(label, axis=1) - 1.0
    total = own_sum[...] + dot(member(label.astype(I32), count), hidden[...])
    fine_sum = dot(total.astype(BF16), w_out[...])
    new = (mids[...].astype(F32) + layer_norm(fine_sum, gain[...])).astype(BF16)
    update[...] = new
    rel = relative_owner(owner[...], lax.axis_index("dev"), members)
    place = places(rel, members, (0, 1, 2, 3), 128)
    slots = 4 * mid_capacity
    labels = flat_row(parent[...]).astype(F32) + 1.0
    picked, marks = [], jnp.zeros((slots, 128), F32)
    for j, part in enumerate(place):
        base = iota((8, 128), 0).astype(F32) * float(mid_capacity)
        slot = jnp.max(jnp.where(part >= 0, part + base, -1.0), axis=0, keepdims=True)
        slot_row[:, 128 * j : 128 * (j + 1)] = jnp.broadcast_to(slot.astype(I32), (8, 128))
        hit = jnp.where(slot == iota((slots, 128), 0).astype(F32), 1.0, 0.0)
        picked.append(hit.astype(BF16))
        marks = marks + hit * labels[:, 128 * j : 128 * (j + 1)]
    marks = jnp.concatenate([marks, jnp.zeros((384 - slots, 128), F32)], axis=0)
    code = digits(jnp.sum(jnp.transpose(marks), axis=0, keepdims=True))
    out = dot(jnp.concatenate(picked, axis=1), new).astype(BF16)
    for c, p in enumerate((p0, p1, p2, p3)):
        p[0:mid_capacity, :] = out[mid_capacity * c : mid_capacity * (c + 1)]
        p[mid_capacity : mid_capacity + 16, 0:384] = code


def mid_own(owner, parent, update, coarse, w_parent, w_child, bias, total, terms, *, members):
    terms[...] = dot(coarse[...], w_parent[...]).astype(BF16)
    rel = relative_owner(owner[...], lax.axis_index("dev"), members)
    label = jnp.where(rel == 0, flat_row(parent[...]), -1)
    count = terms.shape[0]
    before = dot(update[...], w_child[...]) + dot(pick(columns_of(label), count), terms[...]) + bias[...]
    total[...] = dot(member(label, count), silu(before).astype(BF16))


def mid_received(m0, m1, m2, m3, terms, own_sum, w_child, bias, *rest, groups, capacity):
    shares, labels, rows, total = rest[:groups], rest[groups], rest[groups + 1], rest[groups + 2]
    count = terms.shape[0]
    lanes = iota((1, 384), 1)
    label = jnp.zeros((1, 384), F32)
    for c, m in enumerate((m0, m1, m2, m3)):
        rows[capacity * c : capacity * (c + 1), :] = m[0:capacity, :]
        row = undigits(m[capacity : capacity + 16, 0:384])
        mine = (lanes >= capacity * c) & (lanes < capacity * (c + 1))
        label = label + jnp.where(mine, row, 0.0)
    label = (label - 1.0).astype(I32)
    labels[...] = jnp.broadcast_to(label, labels.shape)
    slots = 4 * capacity
    cols = columns_of(label)[0:slots]
    before = dot(rows[...], w_child[...]) + dot(pick(cols, count), terms[...]) + bias[...]
    total[...] = own_sum[...] + dot(member(label[:, 0:slots], count), silu(before).astype(BF16))
    share = count // groups
    for j, out in enumerate(shares):
        at = share_at(j, groups) * share
        out[...] = total[pl.ds(pl.multiple_of(at, 16), share), :].astype(BF16)


def coarse_mine(*refs, pieces):
    pieces, refs = refs[:pieces], refs[pieces:]
    coarse, w_out, gain, w_self, w_other, bias, update, own_terms, other = refs
    total = pieces[0][...].astype(F32)
    for p in pieces[1:]:
        total = total + p[...].astype(F32)
    coarse_sum = dot(total.astype(BF16), w_out[...])
    share = update.shape[0]
    at = pl.multiple_of(lax.axis_index("grp") * share, 16)
    new = (coarse[pl.ds(at, share), :].astype(F32) + layer_norm(coarse_sum, gain[...])).astype(BF16)
    update[...] = new
    other[...] = dot(new, w_other[...]).astype(BF16)
    own_terms[...] = dot(new, w_self[...]) + bias[...]


def same_near(*refs, groups, members):
    pieces = refs[:groups]
    low_first, high_first, low, high, near, mask, found, far_hot, used, window, turned = refs[groups:]
    share = pieces[0].shape[0]
    half, count = groups // 2, groups * share
    part = half * share
    for j, piece in enumerate(pieces):
        at = part + share_at(j, groups) * share
        window[pl.ds(pl.multiple_of(at, 16), share), :] = piece[...]
    g, d = lax.axis_index("grp"), lax.axis_index("dev")
    side = lax.div(g, half)
    for j in range(half):
        at = pl.multiple_of((share_at(j, groups) - side * half) * share, 16)
        rows = slice(share * (j - 1), share * j)
        window[pl.ds(at, share), :] = low[rows, :] if j else low_first[...]
        window[pl.ds(part + count + at, share), :] = high[rows, :] if j else high_first[...]
    own = pl.ds(pl.multiple_of(g * share, 8), share)
    slots = near.shape[0]
    pad = jnp.zeros((128 - slots, count), I32)
    turned[...] = jnp.transpose(jnp.concatenate([mask[...], pad], axis=0))
    used[...] = turned[own, :].astype(F32)
    turned[...] = jnp.transpose(jnp.concatenate([near[...], pad], axis=0))
    whole = members * count
    rel = turned[own, :] - (d - 1) * count
    rel = jnp.where(rel < 0, rel + whole, rel)
    rel = jnp.where(rel >= whole, rel - whole, rel)
    shift = side * part
    place = jnp.where(rel < count, rel - shift, jnp.where(rel < 2 * count, rel - part, rel - shift - part))
    lost = ((rel < count) & ((place < 0) | (place >= part))) | ((rel >= 2 * count) & ((place < part + count) | (place >= 2 * count)))
    place = jnp.where(lost, -1, place)
    far = rel - jnp.where(side == 0, part, 2 * count)
    for k in range(slots):
        cols = jnp.broadcast_to(far[:, k : k + 1], (share, 128))
        far_hot[share * k : share * (k + 1), :] = pick(cols, part)
        cols = jnp.broadcast_to(place[:, k : k + 1], (share, 128))
        found[share * k : share * (k + 1), :] = dot(pick(cols, window.shape[0]), window[...])


def same_far(*refs, groups, slots):
    far_first, far, found, far_hot, used, own_terms, update, w_out, gain, result, window = refs
    share = result.shape[0]
    half = groups // 2
    side = lax.div(lax.axis_index("grp"), half)
    for j in range(half):
        at = pl.multiple_of((share_at(j, groups) - side * half) * share, 16)
        window[pl.ds(at, share), :] = far[share * (j - 1) : share * j, :] if j else far_first[...]
    hidden = jnp.zeros((share, result.shape[1]), F32)
    for k in range(slots):
        rows = slice(share * k, share * (k + 1))
        got = found[rows, :] + dot(far_hot[rows, :], window[...])
        h = silu(own_terms[...] + got).astype(BF16).astype(F32)
        hidden = hidden + used[:, k : k + 1] * h
    same_sum = dot(hidden.astype(BF16), w_out[...])
    result[...] = (update[...].astype(F32) + layer_norm(same_sum, gain[...])).astype(BF16)


def coarse_joined(*refs, groups, capacity):
    pieces = refs[:groups]
    labels, kept, r0, r1, r2, r3 = refs[groups:]
    share = pieces[0].shape[0]
    for j, p in enumerate(pieces):
        at = share_at(j, groups) * share
        kept[pl.ds(pl.multiple_of(at, 16), share), :] = p[...]
    cols = columns_of(labels[0:1, :])[0 : 4 * capacity]
    rows = dot(pick(cols, kept.shape[0]), kept[...]).astype(BF16)
    for c, r in enumerate((r0, r1, r2, r3)):
        r[...] = rows[capacity * c : capacity * (c + 1)]


def down_ready(owner, parent, slot_row, update, w_child, bias, after, child_terms, own_rows, back, *, coarses, slots, members):
    rel = relative_owner(owner[...], lax.axis_index("dev"), members)
    label = jnp.where(rel == 0, flat_row(parent[...]), -1)
    own_rows[...] = pick(columns_of(label), coarses)
    back[...] = pick(columns_of(slot_row[0:1, :]), back.shape[1])
    child_terms[...] = dot(update[...], w_child[...]) + bias[...]


def down_own(own_rows, coarse, w_parent, child_terms, result, whole):
    whole[...] = coarse[...]
    rows = dot(own_rows[...], coarse[...]).astype(BF16)
    terms = dot(rows, w_parent[...]).astype(BF16).astype(F32)
    result[...] = child_terms[...] + terms


def down_received(r0, r1, r2, r3, back, own_terms, update, w_parent, w_out, gain, result, rows, *, capacity):
    for c, r in enumerate((r0, r1, r2, r3)):
        rows[capacity * c : capacity * (c + 1), :] = r[...]
    slots = 4 * capacity
    terms = dot(rows[...], w_parent[...]).astype(BF16)
    before = own_terms[...] + dot(back[:, 0:slots], terms)
    messages = dot(silu(before).astype(BF16), w_out[...])
    result[...] = (update[...].astype(F32) + layer_norm(messages, gain[...])).astype(BF16)


def shape(rows, width, kind=BF16):
    return jax.ShapeDtypeStruct((rows, width), kind)


def call(body, outs, args, scratch=(), flops=0, outside=(), **static):
    moved = sum(a.size * a.dtype.itemsize for a in (*args, *outs))
    return pl.pallas_call(
        functools.partial(body, **static),
        out_shape=outs,
        in_specs=[
            pl.BlockSpec(memory_space=pltpu.HBM if i in outside else pltpu.VMEM) for i in range(len(args))
        ],
        out_specs=[pl.BlockSpec(memory_space=pltpu.VMEM)] * len(outs),
        scratch_shapes=list(scratch),
        cost_estimate=pl.CostEstimate(flops=flops, bytes_accessed=moved, transcendentals=0),
        compiler_params=pltpu.CompilerParams(vmem_limit_bytes=VMEM_LIMIT),
    )(*[pltpu.with_memory_space_constraint(a, pltpu.HBM) if i in outside else a for i, a in enumerate(args)])


def from_behind(value, axis, steps):
    count = lax.axis_size(axis)
    return lax.ppermute(value, axis, [(s, (s + steps) % count) for s in range(count)])


def spilled(value, axis, c, back=False):
    count = lax.axis_size(axis)
    step = -2 if (c == 0) != back else 2
    pairs = []
    for s in range(count):
        target = (s + step, s ^ 1, s + 1 if s % 2 else s - 1, s + step)[c]
        pairs.append((s, target % count))
    return lax.ppermute(value, axis, pairs)


def on_device(
    fine_nodes, mid_nodes, coarse_nodes, fine_owner, fine_parent, mid_owner, mid_parent, neighbours, neighbour_mask,
    up_child_w, up_parent_w, up_out_w, up_bias, up_gain, mid_child_w, mid_parent_w, mid_out_w, mid_bias, mid_gain,
    same_self_w, same_other_w, same_out_w, same_bias, same_gain, down_child_w, down_parent_w, down_out_w,
    down_bias, down_gain,
):
    groups, members = lax.axis_size("grp"), lax.axis_size("dev")
    everyone = groups * members
    fines, width = fine_nodes.shape
    mids, coarses = mid_nodes.shape[0], coarse_nodes.shape[0]
    capacity, mid_capacity = fines // 8, mids // 8
    share = coarses // groups
    everywhere = ("grp", "dev")

    def row(v):
        return v.reshape(1, v.size)

    f_owner, f_parent = row(fine_owner), fine_parent.reshape(-1, 128)
    m_owner, m_parent = row(mid_owner), mid_parent.reshape(-1, 128)
    half = groups // 2

    def moved(value, source):
        return lax.ppermute(value, "grp", [(source(g // half, g % half), g) for g in range(groups)])

    def across(value):
        return moved(value, lambda h, y: (1 - h) * half + y)

    def around(value, s):
        return moved(value, lambda h, y: h * half + (y + s) % half)

    def gathered(value):
        other = across(value)
        near = [around(value, s) for s in range(1, half)]
        far = {s: around(other, s) for s in (1, 3)}
        far[2] = around(other, 2)
        return [value, *near, other] + [far[s] for s in range(1, half)]

    message = shape(capacity + 16, width)
    work = 2 * capacity * fines * width
    packed, nodes, place, label = call(
        pack_first, [message, shape(fines, width), shape(8, fines, F32), shape(8, fines, F32)],
        (f_owner, f_parent, fine_nodes),
        [pltpu.VMEM(f_owner.shape, I32), pltpu.VMEM(f_parent.shape, I32), pltpu.SemaphoreType.DMA((2 + fines // 512,))],
        work, outside=(0, 1, 2), column=0, everyone=everyone, members=members, capacity=capacity,
    )
    got = {0: spilled(packed, everywhere, 0)}
    for c in (3, 2):
        (packed,) = call(pack_next, [message], (place, label, nodes), (), work, column=c, capacity=capacity)
        got[c] = spilled(packed, everywhere, c)
    packed, mid_copy, w_parent, w_child = call(
        pack_next, [message, shape(mids, width)] + [shape(width, width)] * 2,
        (place, label, nodes, mid_nodes, up_parent_w, up_child_w), [pltpu.SemaphoreType.DMA((3,))],
        work, outside=(3, 4, 5), column=1, capacity=capacity,
    )
    got[1] = spilled(packed, everywhere, 1)
    own_sum, mid_terms = call(
        fine_own, [shape(mids, width, F32), shape(mids, width)],
        (label, nodes, mid_copy, w_parent, w_child, row(up_bias)),
        flops=2 * width * (fines * (width + 2 * mids) + mids * width), tile=1280,
    )

    mid_message = shape(mid_capacity + 16, width)
    mid_update, *packed, slot_row = call(
        fine_received, [shape(mids, width)] + [mid_message] * 4 + [shape(8, mids, I32)],
        (*[got[c] for c in range(4)], mid_terms, own_sum, w_child, row(up_bias), up_out_w, row(up_gain), mid_copy, m_owner, m_parent),
        [pltpu.VMEM((4 * capacity, width), BF16)], 2 * width * (4 * capacity * (width + 2 * mids)),
        members=members, capacity=capacity, mid_capacity=mid_capacity,
    )
    got = [spilled(p, "dev", c) for c, p in enumerate(packed)]

    own_sum, coarse_terms = call(
        mid_own, [shape(coarses, width, F32), shape(coarses, width)],
        (m_owner, m_parent, mid_update, coarse_nodes, mid_parent_w, mid_child_w, row(mid_bias)),
        flops=2 * width * (coarses * width + mids * (width + 2 * coarses)), members=members,
    )
    *shares, labels = call(
        mid_received, [shape(share, width)] * groups + [shape(8, 384, I32)],
        (*got, coarse_terms, own_sum, mid_child_w, row(mid_bias)),
        [pltpu.VMEM((4 * mid_capacity, width), BF16), pltpu.VMEM((coarses, width), F32)],
        2 * width * 4 * mid_capacity * (width + 2 * coarses), groups=groups, capacity=mid_capacity,
    )
    first = [around(shares[half + s], -s) for s in range(1, half)]
    second = [around(shares[s], -s) for s in range(1, half)]
    total = sum(p.astype(F32) for p in (shares[half], *first)).astype(BF16)
    pieces = [shares[0], *second, across(total)]

    coarse_update, self_terms, other_terms = call(
        coarse_mine, [shape(share, width), shape(share, width, F32), shape(share, width)],
        (*pieces, coarse_nodes, mid_out_w, row(mid_gain), same_self_w, same_other_w, row(same_bias)),
        flops=6 * share * width * width, pieces=len(pieces),
    )

    pairs = []
    for g in range(groups):
        step = 1 if g < half else -1
        pairs += [(g * members + d, g * members + (d + step) % members) for d in range(members)]
    low_first, high_first = from_behind(other_terms, "dev", 1), from_behind(other_terms, "dev", -1)
    same = gathered(other_terms)
    far_first = lax.ppermute(same[half], everywhere, pairs)
    near_half = jnp.concatenate(same[1:half], axis=0)
    far_half = jnp.concatenate(same[half + 1 :], axis=0)
    low, high = from_behind(near_half, "dev", 1), from_behind(near_half, "dev", -1)
    far = lax.ppermute(far_half, everywhere, pairs)
    slots = neighbours.shape[1]
    found, far_hot, used = call(
        same_near, [shape(slots * share, width, F32), shape(slots * share, half * share), shape(share, 128, F32)],
        (*same, low_first, high_first, low, high, neighbours.T, neighbour_mask.T),
        [pltpu.VMEM((2 * coarses, width), BF16), pltpu.VMEM((coarses, 128), I32)],
        2 * width * slots * share * 2 * coarses, groups=groups, members=members,
    )
    (coarse_part,) = call(
        same_far, [shape(share, width)],
        (far_first, far, found, far_hot, used, self_terms, coarse_update, same_out_w, row(same_gain)),
        [pltpu.VMEM((coarses // 2, width), BF16)], width * slots * share * coarses, groups=groups, slots=slots,
    )

    parts = gathered(coarse_part)
    mid_slots = 4 * mid_capacity
    child_terms, own_rows, back = call(
        down_ready, [shape(mids, width, F32), shape(mids, coarses), shape(mids, -(-mid_slots // 128) * 128)],
        (m_owner, m_parent, slot_row, mid_update, down_child_w, row(down_bias), other_terms),
        flops=2 * width * mids * width, coarses=coarses, slots=mid_slots, members=members,
    )
    piece = shape(mid_capacity, width)
    kept, *outgoing = call(
        coarse_joined, [shape(coarses, width)] + [piece] * 4, (*parts, labels),
        flops=2 * width * mid_slots * coarses, groups=groups, capacity=mid_capacity,
    )
    returned = [spilled(r, "dev", c, back=True) for c, r in enumerate(outgoing)]
    own_terms, coarse_out = call(
        down_own, [shape(mids, width, F32), shape(coarses, width)], (own_rows, kept, down_parent_w, child_terms),
        flops=2 * width * mids * (coarses + width),
    )
    (mid_out,) = call(
        down_received, [shape(mids, width)],
        (*returned, back, own_terms, mid_update, down_parent_w, down_out_w, row(down_gain)),
        [pltpu.VMEM((mid_slots, width), BF16)], 2 * width * mids * (width + 2 * mid_slots), capacity=mid_capacity,
    )
    return (mid_out, coarse_out)


def solution(mesh):
    nodes = P(("grp", "dev"), None)
    coarse = P("dev", None)
    flat = P(("grp", "dev"))
    in_specs = (nodes, nodes, coarse, nodes, flat, nodes, flat, coarse, coarse) + (P(),) * 20

    return jax.shard_map(on_device, mesh=mesh, in_specs=in_specs, out_specs=(nodes, coarse), check_vma=False)
```

```python
import functools

import jax
import jax.numpy as jnp
from jax import lax
from jax.experimental import pallas as pl
from jax.experimental.pallas import tpu as pltpu
from jax.sharding import PartitionSpec as P


F32 = jnp.float32
BF16 = jnp.bfloat16
I32 = jnp.int32
VMEM_LIMIT = 24 * 1024 * 1024


def dot(a, b):
    return jnp.dot(a, b, preferred_element_type=F32)


def iota(shape, dim):
    return lax.broadcasted_iota(I32, shape, dim)


def flat_row(x):
    return jnp.concatenate([x[j : j + 1, :] for j in range(x.shape[0])], axis=1)


def one_hot(hit):
    return jnp.where(hit, 1.0, 0.0).astype(BF16)


def columns_of(row):
    return jnp.transpose(jnp.broadcast_to(row, (128, row.shape[1])))


def pick(cols, count):
    lanes = iota(cols.shape, 1)
    return jnp.concatenate([one_hot(cols == lanes + 128 * j) for j in range(count // 128)], axis=1)


def member(row, count):
    return one_hot(iota((count, row.shape[1]), 0) == row)


def silu(v):
    half = 0.5 * v
    return half + half * jnp.tanh(half)


def layer_norm(values, gain):
    center = values - jnp.mean(values, axis=-1, keepdims=True)
    spread = jnp.mean(center * center, axis=-1, keepdims=True)
    return center * lax.rsqrt(spread + 1e-05) * gain


def digits(row):
    high = jnp.floor(row * (1.0 / 256.0))
    low = row - 256.0 * high
    wide = (8, row.shape[1])
    return jnp.concatenate([jnp.broadcast_to(high, wide), jnp.broadcast_to(low, wide)], axis=0).astype(BF16)


def undigits(block):
    values = block.astype(F32)
    return values[0:1] * 256.0 + values[8:9]


def share_at(j, groups):
    half = groups // 2
    g = lax.axis_index("grp")
    own = lax.div(g, half)
    side = own if j < half else 1 - own
    return side * half + lax.rem(lax.rem(g, half) + j % half, half)


def relative_owner(owner, me, total):
    rel = owner - me
    return jnp.where(rel < 0, rel + total, rel)


def places(rel, total, columns, chunk):
    lanes = rel.shape[1]
    subl = iota((8, lanes), 0)
    code = jnp.full((8, lanes), -5, I32)
    side = 1 - 2 * lax.rem(lax.axis_index("dev"), 2)
    steps = (-2, side, -side, 2)
    for r, c in enumerate(columns):
        code = jnp.where(subl == r, lax.rem(steps[c] + total, total), code)
    chosen = jnp.where(rel == code, 1.0, 0.0)
    parts = lanes // chunk
    stacked = jnp.concatenate([chosen[:, chunk * j : chunk * (j + 1)] for j in range(parts)], axis=0)
    below = one_hot(iota((chunk, chunk), 0) < iota((chunk, chunk), 1))
    before = dot(stacked.astype(BF16), below)
    totals = jnp.sum(stacked, axis=1, keepdims=True)
    offset = jnp.zeros((8, 1), F32)
    out = []
    for j in range(parts):
        rows = slice(8 * j, 8 * j + 8)
        out.append(jnp.where(stacked[rows] > 0, before[rows] + offset, -1.0))
        offset = offset + totals[rows]
    return out


def my_index(members):
    return lax.axis_index("grp") * members + lax.axis_index("dev")


def start_copies(pairs, sems):
    copies = [pltpu.make_async_copy(a, b, sems.at[i]) for i, (a, b) in enumerate(pairs)]
    for c in copies:
        c.start()
    return copies


def packed_rows(place, label, nodes, out, c, capacity, chunk, waits=()):
    block = 64
    marks = [jnp.zeros((block, 128), F32) for _ in range(capacity // block)]
    total = None
    for j in range(place.shape[1] // chunk):
        lanes = slice(chunk * j, chunk * (j + 1))
        rows = []
        for i in range(capacity // block):
            slots = (iota((block, chunk), 0) + block * i).astype(F32)
            hit = jnp.where(place[:, lanes] == slots, 1.0, 0.0)
            rows.append(hit.astype(BF16))
            hit = hit * label[:, lanes]
            marks[i] = marks[i] + ((hit[:, :128] + hit[:, 128:256]) + (hit[:, 256:384] + hit[:, 384:]))
        if waits:
            waits[j].wait()
        part = dot(jnp.concatenate(rows, axis=0), nodes[lanes, :])
        total = part if total is None else total + part
    spare = [jnp.zeros((64, 128), F32)]
    marks = spare + marks if (capacity * c) % 128 else marks + spare
    row = jnp.sum(jnp.transpose(jnp.concatenate(marks, axis=0)), axis=0, keepdims=True)
    out[0:capacity, :] = total.astype(BF16)
    out[capacity : capacity + 16, 0 : capacity + 64] = digits(row)


def pack_first(owner_in, parent_in, nodes_in, out, nodes, place, label, owner, parent, sems, *, column, everyone, members, capacity):
    chunk = 512
    parts = [pl.ds(chunk * j, chunk) for j in range(nodes.shape[0] // chunk)]
    copies = start_copies([(owner_in, owner), (parent_in, parent), *[(nodes_in.at[p], nodes.at[p]) for p in parts]], sems)
    copies[0].wait()
    copies[1].wait()
    rel = relative_owner(owner[...], my_index(members), everyone)
    for j, part in enumerate(places(rel, everyone, (0, 1, 2, 3), 256)):
        place[:, 256 * j : 256 * (j + 1)] = part
    target = flat_row(parent[...]).astype(F32)
    label[0:1, :] = target + 1.0
    label[1:2, :] = jnp.where(rel == 0, target, -1.0)
    packed_rows(place[column : column + 1, :], label[0:1, :], nodes, out, column, capacity, chunk, copies[2:])


def pack_next(place, label, nodes, *rest, column, capacity):
    count = (len(rest) - 1) // 2
    copies = start_copies(list(zip(rest[:count], rest[count + 1 :])), rest[-1]) if count else []
    packed_rows(place[column : column + 1, :], label[0:1, :], nodes, rest[count], column, capacity, 512)
    for copy in copies:
        copy.wait()


def fine_own(labels, nodes, mids, w_parent, w_child, bias, total, terms, *, tile):
    terms[...] = dot(mids[...], w_parent[...]).astype(BF16)
    count = terms.shape[0]
    total[...] = jnp.zeros_like(total)

    def step(i, _):
        at = pl.multiple_of(i * tile, tile)
        label = labels[1:2, pl.ds(at, tile)].astype(I32)
        before = dot(nodes[pl.ds(at, tile), :], w_child[...]) + dot(pick(columns_of(label), count), terms[...]) + bias[...]
        total[...] += dot(member(label, count), silu(before).astype(BF16))
        return 0

    lax.fori_loop(0, nodes.shape[0] // tile, step, 0)


def fine_received(
    m0, m1, m2, m3, terms, own_sum, w_child, bias, w_out, gain, mids, owner, parent,
    update, p0, p1, p2, p3, slot_row, hidden, *, members, capacity, mid_capacity,
):
    count = terms.shape[0]
    rows = []
    for c, m in enumerate((m0, m1, m2, m3)):
        row = undigits(m[capacity : capacity + 16, 0 : capacity + 64]) - 1.0
        cols = columns_of(row.astype(I32))
        shift = (capacity * c) % 128
        cols = cols[shift : shift + capacity]
        before = dot(m[0:capacity, :], w_child[...]) + dot(pick(cols, count), terms[...]) + bias[...]
        hidden[capacity * c : capacity * (c + 1), :] = silu(before).astype(BF16)
        rows.append(row + 1.0)
    label = []
    for a, b in (rows[0:2], rows[2:4]):
        label += [a[:, :256], a[:, 256:] + b[:, :128], b[:, 128:]]
    label = jnp.concatenate(label, axis=1) - 1.0
    total = own_sum[...] + dot(member(label.astype(I32), count), hidden[...])
    fine_sum = dot(total.astype(BF16), w_out[...])
    new = (mids[...].astype(F32) + layer_norm(fine_sum, gain[...])).astype(BF16)
    update[...] = new
    rel = relative_owner(owner[...], lax.axis_index("dev"), members)
    place = places(rel, members, (0, 1, 2, 3), 128)
    slots = 4 * mid_capacity
    labels = flat_row(parent[...]).astype(F32) + 1.0
    picked, marks = [], jnp.zeros((slots, 128), F32)
    for j, part in enumerate(place):
        base = iota((8, 128), 0).astype(F32) * float(mid_capacity)
        slot = jnp.max(jnp.where(part >= 0, part + base, -1.0), axis=0, keepdims=True)
        slot_row[:, 128 * j : 128 * (j + 1)] = jnp.broadcast_to(slot.astype(I32), (8, 128))
        hit = jnp.where(slot == iota((slots, 128), 0).astype(F32), 1.0, 0.0)
        picked.append(hit.astype(BF16))
        marks = marks + hit * labels[:, 128 * j : 128 * (j + 1)]
    marks = jnp.concatenate([marks, jnp.zeros((384 - slots, 128), F32)], axis=0)
    code = digits(jnp.sum(jnp.transpose(marks), axis=0, keepdims=True))
    out = dot(jnp.concatenate(picked, axis=1), new).astype(BF16)
    for c, p in enumerate((p0, p1, p2, p3)):
        p[0:mid_capacity, :] = out[mid_capacity * c : mid_capacity * (c + 1)]
        p[mid_capacity : mid_capacity + 16, 0:384] = code


def mid_own(owner, parent, update, coarse, w_parent, w_child, bias, total, terms, *, members):
    terms[...] = dot(coarse[...], w_parent[...]).astype(BF16)
    rel = relative_owner(owner[...], lax.axis_index("dev"), members)
    label = jnp.where(rel == 0, flat_row(parent[...]), -1)
    count = terms.shape[0]
    before = dot(update[...], w_child[...]) + dot(pick(columns_of(label), count), terms[...]) + bias[...]
    total[...] = dot(member(label, count), silu(before).astype(BF16))


def mid_received(m0, m1, m2, m3, terms, own_sum, w_child, bias, *rest, groups, capacity):
    shares, labels, rows, total = rest[:groups], rest[groups], rest[groups + 1], rest[groups + 2]
    count = terms.shape[0]
    lanes = iota((1, 384), 1)
    label = jnp.zeros((1, 384), F32)
    for c, m in enumerate((m0, m1, m2, m3)):
        rows[capacity * c : capacity * (c + 1), :] = m[0:capacity, :]
        row = undigits(m[capacity : capacity + 16, 0:384])
        mine = (lanes >= capacity * c) & (lanes < capacity * (c + 1))
        label = label + jnp.where(mine, row, 0.0)
    label = (label - 1.0).astype(I32)
    labels[...] = jnp.broadcast_to(label, labels.shape)
    slots = 4 * capacity
    cols = columns_of(label)[0:slots]
    before = dot(rows[...], w_child[...]) + dot(pick(cols, count), terms[...]) + bias[...]
    total[...] = own_sum[...] + dot(member(label[:, 0:slots], count), silu(before).astype(BF16))
    share = count // groups
    for j, out in enumerate(shares):
        at = share_at(j, groups) * share
        out[...] = total[pl.ds(pl.multiple_of(at, 16), share), :].astype(BF16)


def coarse_mine(*refs, pieces):
    pieces, refs = refs[:pieces], refs[pieces:]
    coarse, w_out, gain, w_self, w_other, bias, update, own_terms, other = refs
    total = pieces[0][...].astype(F32)
    for p in pieces[1:]:
        total = total + p[...].astype(F32)
    coarse_sum = dot(total.astype(BF16), w_out[...])
    share = update.shape[0]
    at = pl.multiple_of(lax.axis_index("grp") * share, 16)
    new = (coarse[pl.ds(at, share), :].astype(F32) + layer_norm(coarse_sum, gain[...])).astype(BF16)
    update[...] = new
    other[...] = dot(new, w_other[...]).astype(BF16)
    own_terms[...] = dot(new, w_self[...]) + bias[...]


def same_near(*refs, groups, members):
    pieces = refs[:groups]
    low_first, high_first, low, high, near, mask, found, far_hot, used, window, turned = refs[groups:]
    share = pieces[0].shape[0]
    half, count = groups // 2, groups * share
    part = half * share
    for j, piece in enumerate(pieces):
        at = part + share_at(j, groups) * share
        window[pl.ds(pl.multiple_of(at, 16), share), :] = piece[...]
    g, d = lax.axis_index("grp"), lax.axis_index("dev")
    side = lax.div(g, half)
    for j in range(half):
        at = pl.multiple_of((share_at(j, groups) - side * half) * share, 16)
        rows = slice(share * (j - 1), share * j)
        window[pl.ds(at, share), :] = low[rows, :] if j else low_first[...]
        window[pl.ds(part + count + at, share), :] = high[rows, :] if j else high_first[...]
    own = pl.ds(pl.multiple_of(g * share, 8), share)
    slots = near.shape[0]
    pad = jnp.zeros((128 - slots, count), I32)
    turned[...] = jnp.transpose(jnp.concatenate([mask[...], pad], axis=0))
    used[...] = turned[own, :].astype(F32)
    turned[...] = jnp.transpose(jnp.concatenate([near[...], pad], axis=0))
    whole = members * count
    rel = turned[own, :] - (d - 1) * count
    rel = jnp.where(rel < 0, rel + whole, rel)
    rel = jnp.where(rel >= whole, rel - whole, rel)
    shift = side * part
    place = jnp.where(rel < count, rel - shift, jnp.where(rel < 2 * count, rel - part, rel - shift - part))
    lost = ((rel < count) & ((place < 0) | (place >= part))) | ((rel >= 2 * count) & ((place < part + count) | (place >= 2 * count)))
    place = jnp.where(lost, -1, place)
    far = rel - jnp.where(side == 0, part, 2 * count)
    for k in range(slots):
        cols = jnp.broadcast_to(far[:, k : k + 1], (share, 128))
        far_hot[share * k : share * (k + 1), :] = pick(cols, part)
        cols = jnp.broadcast_to(place[:, k : k + 1], (share, 128))
        found[share * k : share * (k + 1), :] = dot(pick(cols, window.shape[0]), window[...])


def same_far(*refs, groups, slots):
    far_first, far, found, far_hot, used, own_terms, update, w_out, gain, result, window = refs
    share = result.shape[0]
    half = groups // 2
    side = lax.div(lax.axis_index("grp"), half)
    for j in range(half):
        at = pl.multiple_of((share_at(j, groups) - side * half) * share, 16)
        window[pl.ds(at, share), :] = far[share * (j - 1) : share * j, :] if j else far_first[...]
    hidden = jnp.zeros((share, result.shape[1]), F32)
    for k in range(slots):
        rows = slice(share * k, share * (k + 1))
        got = found[rows, :] + dot(far_hot[rows, :], window[...])
        h = silu(own_terms[...] + got).astype(BF16).astype(F32)
        hidden = hidden + used[:, k : k + 1] * h
    same_sum = dot(hidden.astype(BF16), w_out[...])
    result[...] = (update[...].astype(F32) + layer_norm(same_sum, gain[...])).astype(BF16)


def coarse_joined(*refs, groups, capacity):
    pieces = refs[:groups]
    labels, kept, r0, r1, r2, r3 = refs[groups:]
    share = pieces[0].shape[0]
    for j, p in enumerate(pieces):
        at = share_at(j, groups) * share
        kept[pl.ds(pl.multiple_of(at, 16), share), :] = p[...]
    cols = columns_of(labels[0:1, :])[0 : 4 * capacity]
    rows = dot(pick(cols, kept.shape[0]), kept[...]).astype(BF16)
    for c, r in enumerate((r0, r1, r2, r3)):
        r[...] = rows[capacity * c : capacity * (c + 1)]


def down_ready(owner, parent, slot_row, update, w_child, bias, after, child_terms, own_rows, back, *, coarses, slots, members):
    rel = relative_owner(owner[...], lax.axis_index("dev"), members)
    label = jnp.where(rel == 0, flat_row(parent[...]), -1)
    own_rows[...] = pick(columns_of(label), coarses)
    back[...] = pick(columns_of(slot_row[0:1, :]), back.shape[1])
    child_terms[...] = dot(update[...], w_child[...]) + bias[...]


def down_own(own_rows, coarse, w_parent, child_terms, result, whole):
    whole[...] = coarse[...]
    rows = dot(own_rows[...], coarse[...]).astype(BF16)
    terms = dot(rows, w_parent[...]).astype(BF16).astype(F32)
    result[...] = child_terms[...] + terms


def down_received(r0, r1, r2, r3, back, own_terms, update, w_parent, w_out, gain, result, rows, *, capacity):
    for c, r in enumerate((r0, r1, r2, r3)):
        rows[capacity * c : capacity * (c + 1), :] = r[...]
    slots = 4 * capacity
    terms = dot(rows[...], w_parent[...]).astype(BF16)
    before = own_terms[...] + dot(back[:, 0:slots], terms)
    messages = dot(silu(before).astype(BF16), w_out[...])
    result[...] = (update[...].astype(F32) + layer_norm(messages, gain[...])).astype(BF16)


def shape(rows, width, kind=BF16):
    return jax.ShapeDtypeStruct((rows, width), kind)


def call(body, outs, args, scratch=(), flops=0, outside=(), **static):
    moved = sum(a.size * a.dtype.itemsize for a in (*args, *outs))
    return pl.pallas_call(
        functools.partial(body, **static),
        out_shape=outs,
        in_specs=[
            pl.BlockSpec(memory_space=pltpu.HBM if i in outside else pltpu.VMEM) for i in range(len(args))
        ],
        out_specs=[pl.BlockSpec(memory_space=pltpu.VMEM)] * len(outs),
        scratch_shapes=list(scratch),
        cost_estimate=pl.CostEstimate(flops=flops, bytes_accessed=moved, transcendentals=0),
        compiler_params=pltpu.CompilerParams(vmem_limit_bytes=VMEM_LIMIT),
    )(*[pltpu.with_memory_space_constraint(a, pltpu.HBM) if i in outside else a for i, a in enumerate(args)])


def from_behind(value, axis, steps):
    count = lax.axis_size(axis)
    return lax.ppermute(value, axis, [(s, (s + steps) % count) for s in range(count)])


def spilled(value, axis, c, back=False):
    count = lax.axis_size(axis)
    step = -2 if (c == 0) != back else 2
    pairs = []
    for s in range(count):
        target = (s + step, s ^ 1, s + 1 if s % 2 else s - 1, s + step)[c]
        pairs.append((s, target % count))
    return lax.ppermute(value, axis, pairs)


def on_device(
    fine_nodes, mid_nodes, coarse_nodes, fine_owner, fine_parent, mid_owner, mid_parent, neighbours, neighbour_mask,
    up_child_w, up_parent_w, up_out_w, up_bias, up_gain, mid_child_w, mid_parent_w, mid_out_w, mid_bias, mid_gain,
    same_self_w, same_other_w, same_out_w, same_bias, same_gain, down_child_w, down_parent_w, down_out_w,
    down_bias, down_gain,
):
    groups, members = lax.axis_size("grp"), lax.axis_size("dev")
    everyone = groups * members
    fines, width = fine_nodes.shape
    mids, coarses = mid_nodes.shape[0], coarse_nodes.shape[0]
    capacity, mid_capacity = fines // 8, mids // 8
    share = coarses // groups
    everywhere = ("grp", "dev")

    def row(v):
        return v.reshape(1, v.size)

    f_owner, f_parent = row(fine_owner), fine_parent.reshape(-1, 128)
    m_owner, m_parent = row(mid_owner), mid_parent.reshape(-1, 128)
    half = groups // 2

    def moved(value, source):
        return lax.ppermute(value, "grp", [(source(g // half, g % half), g) for g in range(groups)])

    def across(value):
        return moved(value, lambda h, y: (1 - h) * half + y)

    def around(value, s):
        return moved(value, lambda h, y: h * half + (y + s) % half)

    def gathered(value):
        other = across(value)
        near = {s: around(value, s) for s in (2, 1, 3)}
        far = {s: around(other, s) for s in (2, 1)}
        far[3] = around(other, 3)
        return [value] + [near[s] for s in range(1, half)] + [other] + [far[s] for s in range(1, half)]

    message = shape(capacity + 16, width)
    work = 2 * capacity * fines * width
    packed, nodes, place, label = call(
        pack_first, [message, shape(fines, width), shape(8, fines, F32), shape(8, fines, F32)],
        (f_owner, f_parent, fine_nodes),
        [pltpu.VMEM(f_owner.shape, I32), pltpu.VMEM(f_parent.shape, I32), pltpu.SemaphoreType.DMA((2 + fines // 512,))],
        work, outside=(0, 1, 2), column=0, everyone=everyone, members=members, capacity=capacity,
    )
    got = {0: spilled(packed, everywhere, 0)}
    for c in (3, 2):
        (packed,) = call(pack_next, [message], (place, label, nodes), (), work, column=c, capacity=capacity)
        got[c] = spilled(packed, everywhere, c)
    packed, mid_copy, w_parent, w_child = call(
        pack_next, [message, shape(mids, width)] + [shape(width, width)] * 2,
        (place, label, nodes, mid_nodes, up_parent_w, up_child_w), [pltpu.SemaphoreType.DMA((3,))],
        work, outside=(3, 4, 5), column=1, capacity=capacity,
    )
    got[1] = spilled(packed, everywhere, 1)
    own_sum, mid_terms = call(
        fine_own, [shape(mids, width, F32), shape(mids, width)],
        (label, nodes, mid_copy, w_parent, w_child, row(up_bias)),
        flops=2 * width * (fines * (width + 2 * mids) + mids * width), tile=1280,
    )

    mid_message = shape(mid_capacity + 16, width)
    mid_update, *packed, slot_row = call(
        fine_received, [shape(mids, width)] + [mid_message] * 4 + [shape(8, mids, I32)],
        (*[got[c] for c in range(4)], mid_terms, own_sum, w_child, row(up_bias), up_out_w, row(up_gain), mid_copy, m_owner, m_parent),
        [pltpu.VMEM((4 * capacity, width), BF16)], 2 * width * (4 * capacity * (width + 2 * mids)),
        members=members, capacity=capacity, mid_capacity=mid_capacity,
    )
    got = [spilled(p, "dev", c) for c, p in enumerate(packed)]

    own_sum, coarse_terms = call(
        mid_own, [shape(coarses, width, F32), shape(coarses, width)],
        (m_owner, m_parent, mid_update, coarse_nodes, mid_parent_w, mid_child_w, row(mid_bias)),
        flops=2 * width * (coarses * width + mids * (width + 2 * coarses)), members=members,
    )
    *shares, labels = call(
        mid_received, [shape(share, width)] * groups + [shape(8, 384, I32)],
        (*got, coarse_terms, own_sum, mid_child_w, row(mid_bias)),
        [pltpu.VMEM((4 * mid_capacity, width), BF16), pltpu.VMEM((coarses, width), F32)],
        2 * width * 4 * mid_capacity * (width + 2 * coarses), groups=groups, capacity=mid_capacity,
    )
    first = [around(shares[half + s], -s) for s in (2, 1, 3)]
    second = [around(shares[s], -s) for s in (2, 1, 3)]
    total = sum(p.astype(F32) for p in (shares[half], *first)).astype(BF16)
    pieces = [shares[0], *second, across(total)]

    coarse_update, self_terms, other_terms = call(
        coarse_mine, [shape(share, width), shape(share, width, F32), shape(share, width)],
        (*pieces, coarse_nodes, mid_out_w, row(mid_gain), same_self_w, same_other_w, row(same_bias)),
        flops=6 * share * width * width, pieces=len(pieces),
    )

    pairs = []
    for g in range(groups):
        step = 1 if g < half else -1
        pairs += [(g * members + d, g * members + (d + step) % members) for d in range(members)]
    low_first, high_first = from_behind(other_terms, "dev", 1), from_behind(other_terms, "dev", -1)
    same = gathered(other_terms)
    far_first = lax.ppermute(same[half], everywhere, pairs)
    near_half = jnp.concatenate(same[1:half], axis=0)
    far_half = jnp.concatenate(same[half + 1 :], axis=0)
    low, high = from_behind(near_half, "dev", 1), from_behind(near_half, "dev", -1)
    far = lax.ppermute(far_half, everywhere, pairs)
    slots = neighbours.shape[1]
    found, far_hot, used = call(
        same_near, [shape(slots * share, width, F32), shape(slots * share, half * share), shape(share, 128, F32)],
        (*same, low_first, high_first, low, high, neighbours.T, neighbour_mask.T),
        [pltpu.VMEM((2 * coarses, width), BF16), pltpu.VMEM((coarses, 128), I32)],
        2 * width * slots * share * 2 * coarses, groups=groups, members=members,
    )
    (coarse_part,) = call(
        same_far, [shape(share, width)],
        (far_first, far, found, far_hot, used, self_terms, coarse_update, same_out_w, row(same_gain)),
        [pltpu.VMEM((coarses // 2, width), BF16)], width * slots * share * coarses, groups=groups, slots=slots,
    )

    parts = gathered(coarse_part)
    mid_slots = 4 * mid_capacity
    child_terms, own_rows, back = call(
        down_ready, [shape(mids, width, F32), shape(mids, coarses), shape(mids, -(-mid_slots // 128) * 128)],
        (m_owner, m_parent, slot_row, mid_update, down_child_w, row(down_bias), other_terms),
        flops=2 * width * mids * width, coarses=coarses, slots=mid_slots, members=members,
    )
    piece = shape(mid_capacity, width)
    kept, *outgoing = call(
        coarse_joined, [shape(coarses, width)] + [piece] * 4, (*parts, labels),
        flops=2 * width * mid_slots * coarses, groups=groups, capacity=mid_capacity,
    )
    returned = [spilled(r, "dev", c, back=True) for c, r in enumerate(outgoing)]
    own_terms, coarse_out = call(
        down_own, [shape(mids, width, F32), shape(coarses, width)], (own_rows, kept, down_parent_w, child_terms),
        flops=2 * width * mids * (coarses + width),
    )
    (mid_out,) = call(
        down_received, [shape(mids, width)],
        (*returned, back, own_terms, mid_update, down_parent_w, down_out_w, row(down_gain)),
        [pltpu.VMEM((mid_slots, width), BF16)], 2 * width * mids * (width + 2 * mid_slots), capacity=mid_capacity,
    )
    return (mid_out, coarse_out)


def solution(mesh):
    nodes = P(("grp", "dev"), None)
    coarse = P("dev", None)
    flat = P(("grp", "dev"))
    in_specs = (nodes, nodes, coarse, nodes, flat, nodes, flat, coarse, coarse) + (P(),) * 20

    return jax.shard_map(on_device, mesh=mesh, in_specs=in_specs, out_specs=(nodes, coarse), check_vma=False)
```
